32 devices in a mesh: rows: 8 (over z, y), seq: 4 (over x, core).
Axes of the slice: x: 2, y: 2, z: 4, core: 2. Of those that a mesh axis runs over, the one named last changes fastest.
Arguments:
- layer_input: bfloat16 [16, 512, 768], P('rows', 'seq'), may hold values from -6 to 6
- memory: bfloat16 [16, 512, 768], P('rows', 'seq'), may hold values from -6 to 6
- output_grad: bfloat16 [16, 512, 768], P('rows', 'seq'), may hold values from -6 to 6
- segments: int32 [16, 512], P('rows'), may hold values from 0 to 3, never falling along the last dimension, each value on 1 to 256 neighbouring positions
- buckets: int32 [512], replicated, may hold values from 0 to 31, as said below
- self_query: bfloat16 [768, 768], P('rows', 'seq'), may hold values from -0.21875 to 0.21875
- self_key: bfloat16 [768, 768], P('rows', 'seq'), may hold values from -0.21875 to 0.21875
- self_value: bfloat16 [768, 768], P('rows', 'seq'), may hold values from -0.21875 to 0.21875
- self_output: bfloat16 [768, 768], P('rows', 'seq'), may hold values from -1.25 to 1.25
- cross_query: bfloat16 [768, 768], P('rows', 'seq'), may hold values from -0.21875 to 0.21875
- cross_key: bfloat16 [768, 768], P('rows', 'seq'), may hold values from -0.21875 to 0.21875
- cross_value: bfloat16 [768, 768], P('rows', 'seq'), may hold values from -0.21875 to 0.21875
- cross_output: bfloat16 [768, 768], P('rows', 'seq'), may hold values from -1.75 to 1.75
- gate_weight: bfloat16 [768, 2048], P('rows', 'seq'), may hold values from -0.21875 to 0.21875
- up_weight: bfloat16 [768, 2048], P('rows', 'seq'), may hold values from -0.21875 to 0.21875
- down_weight: bfloat16 [2048, 768], P('rows', 'seq'), may hold values from -0.125 to 0.125
- norm_gains: bfloat16 [3, 768], P(None, 'rows'), may hold values from 0.5 to 1.5
- position_bias: bfloat16 [32, 12], replicated, may hold values from -3 to 3
Outputs:
- mixed: bfloat16 [16, 512, 768], P('rows', 'seq')
- input_grad: float32 [16, 512, 768], P('rows', 'seq')
- memory_grad: float32 [16, 512, 768], P('rows', 'seq')
- self_query_grad: float32 [768, 768], P('rows', 'seq')
- self_key_grad: float32 [768, 768], P('rows', 'seq')
- self_value_grad: float32 [768, 768], P('rows', 'seq')
- self_output_grad: float32 [768, 768], P('rows', 'seq')
- cross_query_grad: float32 [768, 768], P('rows', 'seq')
- cross_key_grad: float32 [768, 768], P('rows', 'seq')
- cross_value_grad: float32 [768, 768], P('rows', 'seq')
- cross_output_grad: float32 [768, 768], P('rows', 'seq')
- gate_weight_grad: float32 [768, 2048], P('rows', 'seq')
- up_weight_grad: float32 [768, 2048], P('rows', 'seq')
- down_weight_grad: float32 [2048, 768], P('rows', 'seq')
- norm_gains_grad: float32 [3, 768], P(None, 'rows')
- position_bias_grad: float32 [32, 12], replicated
The draws below stay inside these ranges and needn't reach their ends.
Inputs may be any that keep to these rules, and one draw needn't show every extreme that they name: `segments`: segment ids never fall along a row, every id of 0 to 3 is used, and a document spans 1 to 256 positions. buckets[d] = d for d < 16; the table never falls and buckets[511] = 31.
All inputs are finite; a program needn't handle non-finite values.
Results may differ from the reference program's by a relative error of at most 0.03.
Values may be sent and summed in bfloat16 or wider, within the bound.
A program may use at most 192 MiB of HBM per device.

```python
import math
import jax
import jax.numpy as jnp
import numpy as np
from jax import lax

D = 768
HEADS = 12
HEAD_DIM = 64
FF = 2048
BUCKETS = 32
SEQ_LEN = 512
MEM_LEN = 512
DOCS = 4
MICRO = 2
ROW_DEV = 1
ROWS = 16
N_ROWS = 8


def draw_buckets(key, part):
    exact = BUCKETS // 2
    places = jnp.arange(SEQ_LEN, dtype=jnp.int32)
    rises = (jax.random.randint(key, (SEQ_LEN,), 0, SEQ_LEN - exact) < BUCKETS - exact).astype(jnp.int32)
    rises = jnp.where(places >= exact, rises, 0)
    later = jnp.minimum(exact - 1 + jnp.cumsum(rises).astype(jnp.int32), BUCKETS - 1)
    table = jnp.where(places < exact, places, later)
    return jnp.where(places == SEQ_LEN - 1, BUCKETS - 1, table).astype(jnp.int32)


def raised(values, rng, source, target, parts, factor):
    def block_of(dim):
        return (jnp.arange(values.shape[dim]) // (values.shape[dim] // parts)).reshape((-1,) + (1,) * (values.ndim - 1 - dim))

    near = jax.random.permutation(rng, parts)[block_of(target)]
    far = (block_of(target) + parts // 2) % parts
    return jnp.where((block_of(source) == near) | (block_of(source) == far), factor * values, values)


def block_levels(stream_key, extent, pieces, smallest, top_value):
    def one(dim, blocks):
        draws = jax.random.uniform(jax.random.fold_in(jax.random.fold_in(stream_key, 6), dim), (blocks,), jnp.float32, smallest / len(pieces), top_value / len(pieces))
        return jnp.repeat(jnp.exp(draws), extent[dim] // blocks).reshape((-1,) + (1,) * (len(extent) - dim - 1))

    loudness = one(*pieces[0])
    for cut in pieces[1:]:
        loudness = loudness * one(*cut)
    return loudness


def length_profile(count, total, limit, slope):
    loads = [(1 << 20) // math.isqrt(grade ** slope) + 1 for grade in range(2, count + 1)]
    surplus, holding = total - limit - (count - 1), [1] * (count - 1)
    while surplus > 0:
        candidates = [i for i in range(count - 1) if holding[i] < limit]
        pool, left = sum([loads[i] for i in candidates]), surplus
        for i in candidates:
            addition = min(limit - holding[i], max(1, left * loads[i] // pool), surplus)
            holding[i] = holding[i] + addition
            surplus = surplus - addition
    return np.array([limit] + holding)


def ragged_sizes(rng, count, total, bound, skew):
    if count == 2:
        one = jax.random.randint(rng, (), max(1, total - bound), min(bound, total - 1) + 1)
        return jnp.stack([one, total - one])
    sizes = jnp.asarray(length_profile(count, total, bound, skew), jnp.int32)
    twos = (count - 1) // 2
    source_of, taker = sizes[1:1 + 2 * twos:2], sizes[2:2 + 2 * twos:2]
    room = jnp.minimum(source_of - 1, bound - taker)
    moved = jax.random.randint(jax.random.fold_in(rng, 1), (twos,), 0, 1 << 20) % (room + 1)
    sizes = sizes.at[1:1 + 2 * twos:2].set(source_of - moved).at[2:2 + 2 * twos:2].set(taker + moved)
    return sizes[jax.random.permutation(jax.random.fold_in(rng, 2), count)]


def normal_values(rng, shape, spread, most, cuts=(), kind=jnp.bfloat16):
    loudness = block_levels(rng, shape, cuts, -0.22, 0.18) if cuts else 1.0
    values = jax.random.normal(rng, shape, jnp.float32) * spread * loudness
    return jnp.minimum(jnp.maximum(values, -most), most).astype(kind)


def bell_draw_with(own_key, extent, deviation, most, split, heavy, kind=jnp.bfloat16):
    result = deviation * jax.random.normal(own_key, extent, jnp.float32)
    if split:
        result = result * block_levels(own_key, extent, split, -0.22, 0.18)
    return jnp.clip(raised(result, jax.random.fold_in(own_key, 3), *heavy), -most, most).astype(kind)


def setup_inputs(seed: int = 0) -> dict:
    splits = jax.random.split(jax.random.key(seed), 19)
    return {
        "layer_input": bell_draw_with(splits[0], (ROWS, SEQ_LEN, D), 1.0, 6.0, ((0, 8), (1, 4)), (0, 2, 8, 2.0)),
        "memory": bell_draw_with(splits[1], (ROWS, MEM_LEN, D), 1.0, 6.0, ((0, 8), (1, 4)), (0, 2, 8, 2.0)),
        "output_grad": normal_values(splits[2], (ROWS, SEQ_LEN, D), 1.0, 6.0, ((0, 8), (1, 4))),
        "segments": jax.vmap(lambda own: jnp.searchsorted(jnp.cumsum(ragged_sizes(own, DOCS, SEQ_LEN, SEQ_LEN // 2, 1)), jnp.arange(SEQ_LEN), side="right"))(jax.random.split(splits[3], ROWS)).reshape((ROWS, SEQ_LEN)).astype(jnp.int32),
        "buckets": draw_buckets(jax.random.fold_in(splits[18], 71), 0),
        "self_query": normal_values(splits[5], (D, D), D ** -0.5, 0.21875, ((0, 8), (1, 4))),
        "self_key": normal_values(splits[6], (D, D), D ** -0.5, 0.21875, ((0, 8), (1, 4))),
        "self_value": normal_values(splits[7], (D, D), D ** -0.5, 0.21875, ((0, 8), (1, 4))),
        "self_output": normal_values(splits[8], (D, D), (D // 32) ** -0.5, 1.25, ((0, 8), (1, 4))),
        "cross_query": normal_values(splits[9], (D, D), D ** -0.5, 0.21875, ((0, 8), (1, 4))),
        "cross_key": normal_values(splits[10], (D, D), D ** -0.5, 0.21875, ((0, 8), (1, 4))),
        "cross_value": normal_values(splits[11], (D, D), D ** -0.5, 0.21875, ((0, 8), (1, 4))),
        "cross_output": normal_values(splits[12], (D, D), (D // 64) ** -0.5, 1.75, ((0, 8), (1, 4))),
        "gate_weight": normal_values(splits[13], (D, FF), D ** -0.5, 0.21875, ((0, 8), (1, 4))),
        "up_weight": normal_values(splits[14], (D, FF), D ** -0.5, 0.21875, ((0, 8), (1, 4))),
        "down_weight": normal_values(splits[15], (FF, D), FF ** -0.5, 0.125, ((0, 8), (1, 4))),
        "norm_gains": jnp.clip(1.0 + 0.1 * jax.random.normal(splits[16], (3, D), jnp.float32), 0.5, 1.5).astype(jnp.bfloat16),
        "position_bias": normal_values(splits[17], (BUCKETS, HEADS), 0.5, 3.0),
    }


@jax.custom_vjp
def low(v):
    return lax.optimization_barrier(v.astype(jnp.bfloat16)).astype(jnp.float32)

@jax.custom_vjp
def low_back(v):
    return v

def low_keep(v):
    return (low(v), None)

def low_pass(kept, grad):
    return (grad,)

def back_keep(v):
    return (v, None)

def back_low(kept, grad):
    return (low(grad),)
low.defvjp(low_keep, low_pass)
low_back.defvjp(back_keep, back_low)
EPS = 1e-06
NEG = -1e+30
PRECISION_HIGH = lax.Precision.HIGHEST

def bidirectional_flag(value):
    return low_back(low(value))

def norm_apply(value, gain):
    return value * lax.rsqrt(lax.optimization_barrier(jnp.mean(value * value, axis=-1, keepdims=True)) + EPS) * gain

def matmul(left, weight):
    return jnp.einsum('rsd,df->rsf', left, weight, precision=PRECISION_HIGH)

def split_heads(value):
    return value.reshape(value.shape[0], value.shape[1], HEADS, HEAD_DIM)

def attend(query, key_all, value_all, bias, allowed):
    scores = jnp.einsum('rqhe,rkhe->rhqk', split_heads(query), split_heads(key_all), precision=PRECISION_HIGH)
    scores = low_back(scores * HEAD_DIM ** (-0.5) + bias)
    scores = jnp.where(allowed, scores, NEG)
    soft_weights = low(jax.nn.softmax(scores, axis=-1))
    combined = jnp.einsum('rhqk,rkhe->rqhe', soft_weights, split_heads(value_all), precision=PRECISION_HIGH)
    return bidirectional_flag(combined.reshape(query.shape))
attend_self = jax.checkpoint(attend)

def attend_plain(query, key_all, value_all):
    return attend(query, key_all, value_all, 0.0, True)
attend_cross = jax.checkpoint(attend_plain)

def layer(x_float, m_float, weight_set, gain_rows, bias_table, seg_block, bucket_grid):
    self_query, self_key, self_value, self_output, cross_query, cross_key, cross_value, cross_output, gate_weight, up_weight, down_weight = weight_set
    normed_a = low(norm_apply(x_float, gain_rows[0]))
    query = bidirectional_flag(matmul(normed_a, self_query))
    key_self = bidirectional_flag(matmul(normed_a, self_key))
    value_self = bidirectional_flag(matmul(normed_a, self_value))
    bias = jnp.transpose(bias_table[bucket_grid], (2, 0, 1))[None]
    places = jnp.arange(SEQ_LEN)
    causal = places[None, :] <= places[:, None]
    allowed = (causal[None] & (seg_block[:, :, None] == seg_block[:, None, :]))[:, None]
    attended = attend_self(query, key_self, value_self, bias, allowed)
    x_one = x_float + low_back(matmul(attended, self_output))
    normed_b = low(norm_apply(x_one, gain_rows[1]))
    cross_q = bidirectional_flag(matmul(normed_b, cross_query))
    mem_key = bidirectional_flag(matmul(m_float, cross_key))
    mem_value = bidirectional_flag(matmul(m_float, cross_value))
    cross_att = attend_cross(cross_q, mem_key, mem_value)
    x_two = x_one + low_back(matmul(cross_att, cross_output))
    normed_c = low(norm_apply(x_two, gain_rows[2]))
    gate_pre = low_back(matmul(normed_c, gate_weight))
    up_pre = low_back(matmul(normed_c, up_weight))
    hidden = low(jax.nn.gelu(gate_pre, approximate=True) * up_pre)
    return x_two + low_back(matmul(hidden, down_weight))

def reference(layer_input, memory, output_grad, segments, buckets, self_query, self_key, self_value, self_output, cross_query, cross_key, cross_value, cross_output, gate_weight, up_weight, down_weight, norm_gains, position_bias):
    weight_set = tuple((w.astype(jnp.float32) for w in (self_query, self_key, self_value, self_output, cross_query, cross_key, cross_value, cross_output, gate_weight, up_weight, down_weight)))
    gain_rows = norm_gains.astype(jnp.float32)
    bias_table = position_bias.astype(jnp.float32)
    places = jnp.arange(SEQ_LEN, dtype=jnp.int32)
    bucket_grid = buckets[jnp.maximum(places[:, None] - places[None, :], 0)]
    group = ROW_DEV * MICRO

    def grouped(value):
        return value.reshape((N_ROWS, group) + value.shape[1:])

    def group_step(totals, block_in):
        x_block, m_block, g_block, s_block = block_in

        def forward(x_float, m_float, weights_in, gains_in, table_in):
            return layer(x_float, m_float, weights_in, gains_in, table_in, s_block, bucket_grid)
        primal, pull_back = jax.vjp(forward, x_block.astype(jnp.float32), m_block.astype(jnp.float32), weight_set, gain_rows, bias_table)
        grad_x, grad_m, grad_w, grad_g, grad_b = pull_back(g_block.astype(jnp.float32))
        summed_w = tuple((a + b for a, b in zip(totals[0], grad_w)))
        return ((summed_w, totals[1] + grad_g, totals[2] + grad_b), (primal.astype(jnp.bfloat16), grad_x, grad_m))
    start = (tuple((jnp.zeros_like(w) for w in weight_set)), jnp.zeros_like(gain_rows), jnp.zeros_like(bias_table))
    totals, results = lax.scan(group_step, start, (grouped(layer_input), grouped(memory), grouped(output_grad), grouped(segments)))
    mixed = results[0].reshape(ROWS, SEQ_LEN, D)
    input_grad = results[1].reshape(ROWS, SEQ_LEN, D)
    memory_grad = results[2].reshape(ROWS, MEM_LEN, D)
    wgrads = totals[0]
    return (mixed, input_grad, memory_grad, wgrads[0], wgrads[1], wgrads[2], wgrads[3], wgrads[4], wgrads[5], wgrads[6], wgrads[7], wgrads[8], wgrads[9], wgrads[10], totals[1], totals[2])
```

```python
import jax
import jax.numpy as jnp
from jax import lax
from jax.experimental import pallas as pl
from jax.experimental.pallas import tpu as pltpu
from jax.sharding import PartitionSpec as P

HEADS = 12
BUCKETS = 32
EPS = 1e-06
NEG = -1e30
F32 = jnp.float32
BF16 = jnp.bfloat16
MESH = pl.DeviceIdType.MESH
T = 512
D = 768
H = 384
FH = 1024
VMEM = pltpu.VMEM


def dotf(a, b):
    return jnp.dot(a, b, preferred_element_type=F32)


def dot_t(a, b):
    return lax.dot_general(a, b, (((1,), (1,)), ((), ())), preferred_element_type=F32)


def repeat(count, body):
    lax.fori_loop(0, count, lambda i, carry: (body(i), carry)[1], 0)


def tile(start, step, size):
    return pl.ds(pl.multiple_of(start * step, step), size)


def rms_scale(v):
    return lax.rsqrt(jnp.mean(v * v, axis=-1, keepdims=True) + EPS)


def norm_back(v, gain, upstream):
    r = rms_scale(v)
    scaled = gain * upstream
    gv = r * scaled - v * (r * r * r) * jnp.mean(scaled * v, axis=-1, keepdims=True)
    return gv, jnp.sum(upstream * v * r, axis=0, keepdims=True)


def layer_kernel(
    inp, segr, segc, table, gains,
    w_qkv, w_o, w_cq, w_ckv, w_co, w_g, w_u, w_d,
    mixed, input_grad, memory_grad, gains_grad, dist_grad,
    g_qkv, g_o, g_cq, g_ckv, g_co, g_g, g_u, g_d,
    full, na, nb, nc, qkv, att, x1, cq, mkv, catt, x2,
    bias, p_self, p_cross, hidden, gg, gu, gsend, grecv, gx2, gxb,
    gatt, gcq, gqkv, dk_t, dv_t, qt_s, gt_s, left_t, work,
    psend, precv, msend, late, gdsend,
    ssem, rsem,
):
    row = lax.axis_index("rows")
    seq = lax.axis_index("seq")
    x = lax.div(seq, 2)
    c = lax.rem(seq, 2)
    mate = (row, 2 * x + (1 - c))
    across = (row, lax.rem(seq + 2, 4))

    barrier = pltpu.get_barrier_semaphore()
    for peer in (mate, across):
        pl.semaphore_signal(barrier, inc=1, device_id=peer, device_id_type=MESH)
    pl.semaphore_wait(barrier, 2)

    started = []

    def remote(src, dst, slot, peer):
        copy = pltpu.make_async_remote_copy(
            src_ref=src, dst_ref=dst, send_sem=ssem.at[slot], recv_sem=rsem.at[slot],
            device_id=peer, device_id_type=MESH)
        copy.start()
        started.append(copy)
        return copy

    mine = tile(c, H, H)
    low = lax.broadcasted_iota(jnp.int32, (1, 128), 1) < 64
    masks = (low, jnp.logical_not(low))
    flip = (
        lax.broadcasted_iota(jnp.int32, (256, 256), 0)
        + lax.broadcasted_iota(jnp.int32, (256, 256), 1)
        == 255
    ).astype(BF16)

    own = tile(seq, 128, 128)
    other = tile(lax.rem(seq + 2, 4), 128, 128)
    to_across = remote(inp.at[:, 1 - x], full.at[:, own], 0, across)
    to_mate = remote(inp.at[:, x], full.at[:, own], 1, mate)
    for k in range(3):
        full[k, own] = inp[k, x]

    for qt in range(2):
        rows = slice(256 * qt, 256 * qt + 256)
        qpos = lax.broadcasted_iota(jnp.int32, (256, T), 0) + 256 * qt
        kpos = lax.broadcasted_iota(jnp.int32, (256, T), 1)
        allowed = (kpos <= qpos) & (segc[rows, :] == segr[...])
        work[0:256] = jnp.where(allowed, 0.0, NEG)

        def build(h):
            line = jnp.broadcast_to(table[pl.ds(h, 1), :], (256, T))
            line = pltpu.roll(line, 256 * qt, 1, stride=1, stride_axis=0)
            bias[h, rows] = (line + work[0:256]).astype(BF16)

        repeat(6, build)

    to_across.wait_recv()
    relay = remote(full.at[:, other], full.at[:, other], 2, mate)
    to_mate.wait_recv()
    relay.wait_recv()

    def norm(source, gain, dest):
        def part(i):
            chunk = tile(i, 128, 128)
            v = source(chunk)
            dest[chunk] = (v * rms_scale(v) * gains[gain : gain + 1]).astype(BF16)

        repeat(4, part)

    norm(lambda k: full[0, k].astype(F32), 0, na)

    def project_qkv(n):
        cols = tile(n, H, H)
        qkv[:, cols] = (dotf(na[...], w_qkv[:, cols]).astype(BF16) * jnp.where(n == 0, 0.125, 1.0)).astype(BF16)

    repeat(3, project_qkv)

    def attend(t, q, qo, k, ko, v, vo, bias_ref, probs, out):
        qc, kc, vc = tile(t + qo, 128, 128), tile(t + ko, 128, 128), tile(t + vo, 128, 128)
        oc = tile(t + 3 * c, 128, 128)
        for qt in range(2):
            rows = slice(256 * qt, 256 * qt + 256)
            nk = T if bias_ref is None else 256 * (qt + 1)
            q2, k2, v2 = q[rows, qc], k[0:nk, kc], v[0:nk, vc]
            outs = []
            for a in range(2):
                s = dot_t(jnp.where(masks[a], q2, jnp.zeros_like(q2)), k2)
                if bias_ref is not None:
                    s = s + bias_ref[2 * t + a, rows, 0:nk].astype(F32)
                e = jnp.exp(s - jnp.max(s, axis=-1, keepdims=True))
                prob = (e * (1.0 / jnp.sum(e, axis=-1, keepdims=True))).astype(BF16)
                probs[2 * t + a, rows, 0:nk] = prob
                outs.append(dotf(prob, v2))
            out[rows, oc] = jnp.where(low, outs[0], outs[1]).astype(BF16)

    def attend_back(t, q, qo, k, ko, v, vo, probs, out, causal, gq, gqo, gk, gko, gv, gvo):
        qc, kc, vc = tile(t + qo, 128, 128), tile(t + ko, 128, 128), tile(t + vo, 128, 128)
        oc, gc = tile(t + 3 * c, 128, 128), tile(t, 128, 128)
        qt_s[...] = q[:, qc].T
        gt_s[...] = gatt[:, gc].T
        for qt in (1, 0):
            rows = slice(256 * qt, 256 * qt + 256)
            nk = 256 * (qt + 1) if causal else T
            k2, v2 = k[0:nk, kc], v[0:nk, vc]
            g2 = gatt[rows, gc]
            both = g2.astype(F32) * out[rows, oc].astype(F32)
            outs = []
            for a in range(2):
                half = slice(64 * a, 64 * a + 64)
                delta = jnp.sum(jnp.where(masks[a], both, 0.0), axis=-1, keepdims=True)
                dp = dot_t(jnp.where(masks[a], g2, jnp.zeros_like(g2)), v2)
                prob = probs[2 * t + a, rows, 0:nk]
                ds = (prob.astype(F32) * (dp - delta)).astype(BF16)
                outs.append(dotf(ds, k2))
                dk = dotf(qt_s[half, rows], ds)
                dv = dotf(gt_s[half, rows], prob)
                if qt == 1:
                    dk_t[half, :] = dk
                    dv_t[half, :] = dv
                else:
                    dk_t[half, 0:nk] += dk
                    dv_t[half, 0:nk] += dv
                if causal:
                    band = slice(256 * a, 256 * a + 256)
                    if qt == 1:
                        work[band] = dotf(flip, ds)
                    else:
                        work[band, 256:T] += dotf(flip, ds)
                        turned = pltpu.roll(work[band], 0, 1, stride=1, stride_axis=0)
                        dist_grad[pl.ds(2 * t + a, 1), :] = jnp.sum(turned, axis=0, keepdims=True)
            gq[rows, tile(t + gqo, 128, 128)] = (jnp.where(low, outs[0], outs[1]) * 0.125).astype(BF16)
        gk[:, tile(t + gko, 128, 128)] = dk_t[...].T.astype(BF16)
        gv[:, tile(t + gvo, 128, 128)] = dv_t[...].T.astype(BF16)

    def send_head(ref, t, slot):
        cols = tile(t + 3 * c, 128, 128)
        return remote(ref.at[:, cols], ref.at[:, cols], slot + t, mate)

    def wait_all(copies):
        for copy in copies:
            copy.wait_recv()

    copies = []
    for t in range(3):
        attend(t, qkv, 0, qkv, 3, qkv, 6, bias, p_self, att)
        copies.append(send_head(att, t, 3))

    def project_memory(n):
        cols = tile(n, 256, 256)
        mkv[:, cols] = dotf(full[1], w_ckv[:, cols]).astype(BF16)

    repeat(3, project_memory)
    wait_all(copies)

    def first_residual(n):
        cols = tile(n, 256, 256)
        x1[:, cols] = full[0, :, cols].astype(F32) + dotf(att[...], w_o[:, cols])

    repeat(3, first_residual)
    norm(lambda k: x1[k], 1, nb)
    cq[...] = (dotf(nb[...], w_cq[:, mine]).astype(BF16) * 0.125).astype(BF16)

    copies = []
    for t in range(3):
        attend(t, cq, 0, mkv, 0, mkv, 3, None, p_cross, catt)
        copies.append(send_head(catt, t, 6))
    wait_all(copies)

    def second_residual(n):
        cols = tile(n, 256, 256)
        x2[:, cols] = x1[:, cols] + dotf(catt[...], w_co[:, cols])

    repeat(3, second_residual)
    norm(lambda k: x2[k], 2, nc)

    def feed(n):
        cols = tile(n, 256, 256)
        gate = dotf(nc[...], w_g[:, cols])
        up = dotf(nc[...], w_u[:, cols])
        back = dot_t(full[2], w_d[cols, :])
        square = gate * gate
        th = jnp.tanh(0.7978845608028654 * gate * (1.0 + 0.044715 * square))
        half = 0.5 * (1.0 + th)
        act = gate * half
        slope = half + 0.5 * gate * (1.0 - th * th) * (0.7978845608028654 * (1.0 + 0.134145 * square))
        hidden[:, cols] = (act * up).astype(BF16)
        gg[:, cols] = (back * up * slope).astype(BF16)
        gu[:, cols] = (back * act).astype(BF16)

    repeat(4, feed)

    gc_copies = []
    for n in range(3):
        cols = slice(256 * n, 256 * n + 256)
        gsend[:, cols] = (dot_t(gg[...], w_g[cols, :]) + dot_t(gu[...], w_u[cols, :])).astype(BF16)
        gc_copies.append(remote(gsend.at[:, cols], grecv.at[:, cols], 9 + n, mate))

    def pair_partial(product, buf_send, buf_recv, slot):
        def part(n):
            cols = tile(n, 256, 256)
            value = product(cols).astype(BF16)
            for b in range(4):
                buf_send[b, :, cols] = value[128 * b : 128 * b + 128]

        repeat(3, part)
        return [remote(buf_send.at[2 * k + (1 - c)], buf_recv.at[k], slot + k, mate) for k in range(2)]

    mix_copies = pair_partial(lambda k: dotf(hidden[...], w_d[:, k]), psend.at[0], precv.at[0], 12)

    def weight_grad(left, left_rows, grads):
        def turn(j):
            left_t[tile(j, 128, 128), :] = left(tile(j, 128, 128)).T

        repeat(left_rows // 128, turn)
        for grad, dest, count in grads:
            def part(n):
                dest(n, dotf(left_t[0:left_rows], grad(n)).astype(BF16))

            repeat(count, part)

    def into(ref):
        def put(n, value):
            ref[:, tile(n, 128, 128)] = value
        return put

    def cols_of(ref, first=0):
        return lambda n: ref[:, tile(n + first, 128, 128)]

    weight_grad(lambda j: nc[:, j], D, [(cols_of(gg), into(g_g), 8), (cols_of(gu), into(g_u), 8)])

    def put_own(n, value):
        g_d[tile(c, FH, FH), tile(n, 128, 128)] = value

    def put_mate(n, value):
        gdsend[:, tile(n, 128, 128)] = value

    weight_grad(lambda j: hidden[:, j], FH, [
        (lambda n: full[2, :, tile(n + 3 * (1 - c), 128, 128)], put_mate, 3),
        (lambda n: full[2, :, tile(n + 3 * c, 128, 128)], put_own, 3),
    ])
    gd_copy = remote(gdsend, g_d.at[tile(c, FH, FH)], 24, mate)

    wait_all(gc_copies)
    gains_grad[...] = jnp.zeros_like(gains_grad)

    def keep_gain(index, i, gain):
        gains_grad[index : index + 1] += jnp.where(lax.rem(i, 2) == c, gain, 0.0)

    def third(i):
        chunk = tile(i, 128, 128)
        upstream = gsend[chunk].astype(F32) + grecv[chunk].astype(F32)
        gv, gain = norm_back(x2[chunk], gains[2:3], upstream)
        total = full[2, chunk].astype(F32) + gv
        gx2[chunk] = total
        gxb[chunk] = total.astype(BF16)
        keep_gain(2, i, gain)

    repeat(4, third)
    gatt[...] = dot_t(gxb[...], w_co[mine, :]).astype(BF16)
    gmkv = grecv
    copies = []
    for t in range(3):
        attend_back(t, cq, 0, mkv, 0, mkv, 3, p_cross, catt, False, gcq, 3 * c, gmkv, 0, gmkv, 3)
        copies.append(send_head(gcq, t, 14))

    mem_copies = pair_partial(lambda k: dot_t(gmkv[...], w_ckv[k, :]), psend.at[1], precv.at[1], 17)

    wait_all(mix_copies)

    def mixed_block(k, chunk):
        return (x2[chunk] + psend[0, 2 * k + c].astype(F32) + precv[0, k].astype(F32)).astype(BF16)

    msend[0] = mixed_block(1 - x, other)
    mix_out = remote(msend.at[0], mixed.at[x], 19, across)
    mixed[x] = mixed_block(x, own)

    weight_grad(lambda j: catt[:, j], D, [(cols_of(gxb, 3 * c), into(g_co), 3)])
    wait_all(copies)

    def back_b(n):
        cols = tile(n, 256, 256)
        x2[:, cols] = dot_t(gcq[...], w_cq[cols, :])

    repeat(3, back_b)

    def second(i):
        chunk = tile(i, 128, 128)
        gv, gain = norm_back(x1[chunk], gains[1:2], x2[chunk])
        total = gx2[chunk] + gv
        gx2[chunk] = total
        gxb[chunk] = total.astype(BF16)
        keep_gain(1, i, gain)

    repeat(4, second)
    gatt[...] = dot_t(gxb[...], w_o[mine, :]).astype(BF16)
    for t in range(3):
        attend_back(t, qkv, 0, qkv, 3, qkv, 6, p_self, att, True, gqkv, 0, gqkv, 3, gqkv, 6)

    ig_copies = pair_partial(lambda k: dot_t(gqkv[...], w_qkv[k, :]), psend.at[2], precv.at[2], 21)

    weight_grad(lambda j: full[1, :, j], D, [(cols_of(gmkv), into(g_ckv), 6)])
    weight_grad(lambda j: nb[:, j], D, [(cols_of(gcq, 3 * c), into(g_cq), 3)])
    weight_grad(lambda j: att[:, j], D, [(cols_of(gxb, 3 * c), into(g_o), 3)])
    weight_grad(lambda j: na[:, j], D, [(cols_of(gqkv), into(g_qkv), 9)])

    wait_all(mem_copies)
    msend[1] = (psend[1, 2 * (1 - x) + c].astype(F32) + precv[1, 1 - x].astype(F32)).astype(BF16)
    mem_out = remote(msend.at[1], late.at[0], 20, across)
    memory_grad[x] = psend[1, 2 * x + c].astype(F32) + precv[1, x].astype(F32)

    wait_all(ig_copies)

    def first_block(k, chunk):
        upstream = psend[2, 2 * k + c].astype(F32) + precv[2, k].astype(F32)
        gv, gain = norm_back(full[0, chunk].astype(F32), gains[0:1], upstream)
        gains_grad[0:1] += gain
        return gx2[chunk] + gv

    msend[2] = first_block(1 - x, other).astype(BF16)
    ig_out = remote(msend.at[2], late.at[1], 23, across)
    input_grad[x] = first_block(x, own)

    mem_out.wait_recv()
    memory_grad[1 - x] = late[0].astype(F32)
    ig_out.wait_recv()
    input_grad[1 - x] = late[1].astype(F32)
    mix_out.wait_recv()
    gd_copy.wait_recv()
    for copy in started:
        copy.wait_send()


def layer(inp, segr, segc, table, gains, weights):
    def bf(*shape):
        return VMEM(shape, BF16)

    def fl(*shape):
        return VMEM(shape, F32)

    outs = [
        ((2, 128, D), BF16), ((2, 128, D), F32), ((2, 128, D), F32), ((8, D), F32), ((8, T), F32),
        ((D, 3 * H), BF16), ((D, H), BF16), ((D, H), BF16), ((D, D), BF16), ((D, H), BF16),
        ((D, FH), BF16), ((D, FH), BF16), ((2 * FH, H), BF16),
    ]
    whole = pl.BlockSpec(memory_space=pltpu.VMEM)
    return pl.pallas_call(
        layer_kernel,
        out_shape=[jax.ShapeDtypeStruct(s, d) for s, d in outs],
        in_specs=[whole] * (5 + len(weights)),
        out_specs=[whole] * len(outs),
        scratch_shapes=[
            bf(3, T, D), bf(T, D), bf(T, D), bf(T, D), bf(T, 3 * H), bf(T, D), fl(T, D), bf(T, H), bf(T, D),
            bf(T, D), fl(T, D),
            bf(6, T, T), bf(6, T, T), bf(6, T, T), bf(T, FH), bf(T, FH), bf(T, FH), bf(T, D), bf(T, D),
            fl(T, D), bf(T, D),
            bf(T, H), bf(T, D), bf(T, 3 * H), fl(128, T), fl(128, T), bf(128, T), bf(128, T),
            bf(FH, T), fl(T, T),
            bf(3, 4, 128, D), bf(3, 2, 128, D), bf(3, 128, D), bf(2, 128, D), bf(FH, H),
            pltpu.SemaphoreType.DMA((25,)), pltpu.SemaphoreType.DMA((25,)),
        ],
        compiler_params=pltpu.CompilerParams(
            collective_id=0, has_side_effects=True, vmem_limit_bytes=67043328),
        name="layer",
    )(inp, segr, segc, table, gains, *weights)


def to_plane(v, axis):
    axis = axis % v.ndim
    s = v.shape
    v = v.reshape(s[:axis] + (2, 2, 3, 64) + s[axis + 1 :])
    order = list(range(axis)) + [axis + 1, axis + 2, axis, axis + 3] + list(range(axis + 4, v.ndim))
    return v.transpose(order).reshape(s)


def from_plane(v, axis):
    axis = axis % v.ndim
    s = v.shape
    v = v.reshape(s[:axis] + (2, 3, 2, 64) + s[axis + 1 :])
    order = list(range(axis)) + [axis + 2, axis, axis + 1, axis + 3] + list(range(axis + 4, v.ndim))
    return v.transpose(order).reshape(s)


def ff_plane(v, axis):
    axis = axis % v.ndim
    s = v.shape
    v = v.reshape(s[:axis] + (2, 2, 512) + s[axis + 1 :])
    return jnp.swapaxes(v, axis, axis + 1).reshape(s)


def shards(
    layer_input, memory, output_grad, segments, buckets,
    self_query, self_key, self_value, self_output,
    cross_query, cross_key, cross_value, cross_output,
    gate_weight, up_weight, down_weight, norm_gains, position_bias,
):
    seq = lax.axis_index("seq")
    x, c = seq // 2, seq % 2
    mates = [[0, 2], [1, 3]]

    def whole(w):
        return lax.all_gather(lax.all_gather(w, "rows", axis=0, tiled=True), "seq", axis=1, tiled=True)

    def my_cols(w, width):
        return lax.dynamic_slice_in_dim(w, c * width, width, 1)

    square = jnp.stack([self_query, self_key, self_value, self_output, cross_query, cross_key, cross_value, cross_output])
    square = lax.all_gather(lax.all_gather(square, "rows", axis=1, tiled=True), "seq", axis=2, tiled=True)
    square = to_plane(to_plane(square, 1), 2)
    mine = lax.dynamic_slice_in_dim(square, c * H, H, 2)
    w_qkv = jnp.concatenate([mine[0], mine[1], mine[2]], axis=1)
    w_ckv = jnp.concatenate([mine[5], mine[6]], axis=1)
    w_g = my_cols(ff_plane(to_plane(whole(gate_weight), 0), 1), FH)
    w_u = my_cols(ff_plane(to_plane(whole(up_weight), 0), 1), FH)
    w_d = lax.dynamic_slice_in_dim(to_plane(ff_plane(whole(down_weight), 0), 1), c * FH, FH, 0)
    gains = to_plane(lax.all_gather(norm_gains, "rows", axis=1, tiled=True).astype(F32), 1)
    gains = jnp.pad(gains, ((0, 5), (0, 0)))

    inp = to_plane(jnp.stack([layer_input, memory, output_grad]), 3)
    seg = lax.dynamic_slice_in_dim(segments, x, 1, 0)
    turned = jnp.concatenate([buckets[:1], jnp.flip(buckets[1:])])
    ids = jnp.arange(BUCKETS, dtype=jnp.int32)
    onehot = (turned[None] == ids[:, None]).astype(BF16)
    table = lax.dot_general(position_bias, onehot, (((0,), (0,)), ((), ())), preferred_element_type=F32)
    table = lax.dynamic_index_in_dim(table.reshape(2, 2, 3, T), c, 1, keepdims=False)
    table = jnp.pad(table.transpose(1, 0, 2).reshape(6, T), ((0, 2), (0, 0)))

    (mixed, input_grad, memory_grad, gains_grad, dist_grad,
     g_qkv, g_o, g_cq, g_ckv, g_co, g_g, g_u, g_d) = layer(
        inp, seg, seg.reshape(T, 1), table, gains,
        (w_qkv, square[3], square[4], w_ckv, square[7], w_g, w_u, w_d))

    def own_part(grad):
        grad = lax.psum_scatter(grad, "rows", scatter_dimension=0, tiled=True)
        parts = grad.reshape(grad.shape[0], 2, grad.shape[1] // 2).astype(F32)
        kept = lax.dynamic_index_in_dim(parts, x, 1, keepdims=False)
        sent = lax.dynamic_index_in_dim(parts, 1 - x, 1, keepdims=False).astype(BF16)
        back = lax.ppermute(sent, "seq", [(0, 2), (2, 0), (1, 3), (3, 1)])
        return kept + back.astype(F32)

    def square_grad(grad):
        grad = from_plane(grad, 0)
        return own_part(grad.reshape(D, 3, 2, 64).transpose(0, 2, 1, 3).reshape(D, H))

    def wide_grad(grad):
        return own_part(from_plane(grad, 0))

    def down_grad(grad):
        grad = ff_plane(grad, 0)
        return own_part(grad.reshape(2048, 3, 2, 64).transpose(0, 2, 1, 3).reshape(2048, H))

    gains_grad = from_plane(gains_grad[:3], 1)
    rev = (jnp.flip(buckets)[:, None] == ids[None]).astype(F32)
    per_head = jnp.dot(dist_grad[:6], rev, precision=lax.Precision.HIGHEST)
    bias_grad = jnp.zeros((2, 2, 3, BUCKETS), F32)
    mine_grad = per_head.reshape(3, 2, BUCKETS).transpose(1, 0, 2)[:, None]
    bias_grad = lax.dynamic_update_slice_in_dim(bias_grad, mine_grad, c, 1).reshape(HEADS, BUCKETS).T
    bias_grad, gains_grad = lax.psum((bias_grad, gains_grad), ("rows", "seq"))
    width = D // lax.axis_size("rows")
    gains_own = lax.dynamic_slice_in_dim(gains_grad, lax.axis_index("rows") * width, width, 1)
    return (
        from_plane(mixed, 2), from_plane(input_grad, 2), from_plane(memory_grad, 2),
        square_grad(g_qkv[:, :H]), square_grad(g_qkv[:, H : 2 * H]), square_grad(g_qkv[:, 2 * H :]),
        square_grad(g_o), square_grad(g_cq), square_grad(g_ckv[:, :H]), square_grad(g_ckv[:, H:]),
        square_grad(g_co), wide_grad(g_g), wide_grad(g_u), down_grad(g_d),
        gains_own, bias_grad,
    )


def solution(mesh):
    tokens = P("rows", "seq", None)
    weight = P("rows", "seq")
    return jax.shard_map(
        shards,
        mesh=mesh,
        in_specs=(tokens, tokens, tokens, P("rows", None), P()) + (weight,) * 11 + (P(None, "rows"), P()),
        out_specs=(tokens,) * 3 + (weight,) * 11 + (P(None, "rows"), P()),
        check_vma=False,
    )
```

```python
import jax
import jax.numpy as jnp
from jax import lax
from jax.experimental import pallas as pl
from jax.experimental.pallas import tpu as pltpu
from jax.sharding import PartitionSpec as P

HEADS = 12
BUCKETS = 32
EPS = 1e-06
NEG = -1e30
F32 = jnp.float32
BF16 = jnp.bfloat16
MESH = pl.DeviceIdType.MESH
T = 512
D = 768
H = 384
FH = 1024
VMEM = pltpu.VMEM


def dotf(a, b):
    return jnp.dot(a, b, preferred_element_type=F32)


def dot_t(a, b):
    return lax.dot_general(a, b, (((1,), (1,)), ((), ())), preferred_element_type=F32)


def repeat(count, body):
    lax.fori_loop(0, count, lambda i, carry: (body(i), carry)[1], 0)


def tile(start, step, size):
    return pl.ds(pl.multiple_of(start * step, step), size)


def rms_scale(v):
    return lax.rsqrt(jnp.mean(v * v, axis=-1, keepdims=True) + EPS)


def norm_back(v, gain, upstream):
    r = rms_scale(v)
    scaled = gain * upstream
    gv = r * scaled - v * (r * r * r) * jnp.mean(scaled * v, axis=-1, keepdims=True)
    return gv, jnp.sum(upstream * v * r, axis=0, keepdims=True)


def roll_half(v):
    return pltpu.roll(v, 64, 1)


def low_lanes():
    return lax.broadcasted_iota(jnp.int32, (1, 128), 1) < 64


def sliced_order(tiles):
    low = low_lanes()
    out = []
    for n in range(6):
        a, b = tiles[n // 2], tiles[n // 2 + 3]
        out.append(jnp.where(low, a, roll_half(b)) if n % 2 == 0 else jnp.where(low, roll_half(a), b))
    return out


def natural_order(tiles):
    low = low_lanes()
    out = [jnp.where(low, tiles[2 * k], roll_half(tiles[2 * k + 1])) for k in range(3)]
    return out + [jnp.where(low, roll_half(tiles[2 * k]), tiles[2 * k + 1]) for k in range(3)]


def lane_tiles(v):
    return [v[:, 128 * n : 128 * n + 128] for n in range(v.shape[1] // 128)]


def layer_kernel(
    in_x, in_m, in_g, segments, buckets, pos_bias, w_in, wd_in,
    mixed, input_grad, memory_grad, small, gw, gwd,
    w, wd,    w_o, w_cq, w_co, w_d, gains, table, dist_grad, full, ffb, na, qkv, att, attn, x1, cq, mkv, catt, cattn, x2,
    bias, p_self, hidden, gg, gu, gsend, grecv, gx2, gxb,
    gcq, dk_t, dv_t, qt_s, gt_s, left_t, work,
    psend, precv, msend, late, gdsend,
    ssem, rsem,
):
    p_cross = bias
    nb = nc = na
    gatt = hidden
    row = lax.axis_index("rows")
    seq = lax.axis_index("seq")
    x = lax.div(seq, 2)
    c = lax.rem(seq, 2)
    mate = (row, 2 * x + (1 - c))
    across = (row, lax.rem(seq + 2, 4))

    barrier = pltpu.get_barrier_semaphore()
    for peer in (mate, across):
        pl.semaphore_signal(barrier, inc=1, device_id=peer, device_id_type=MESH)
    pl.semaphore_wait(barrier, 2)

    started = []

    def remote(src, dst, slot, peer):
        copy = pltpu.make_async_remote_copy(
            src_ref=src, dst_ref=dst, send_sem=ssem.at[slot], recv_sem=rsem.at[slot],
            device_id=peer, device_id_type=MESH)
        copy.start()
        started.append(copy)
        return copy

    mine = tile(c, H, H)
    low = lax.broadcasted_iota(jnp.int32, (1, 128), 1) < 64
    masks = (low, jnp.logical_not(low))
    flip = (
        lax.broadcasted_iota(jnp.int32, (256, 256), 0)
        + lax.broadcasted_iota(jnp.int32, (256, 256), 1)
        == 255
    ).astype(BF16)

    own = tile(seq, 128, 128)
    other = tile(lax.rem(seq + 2, 4), 128, 128)
    dist_grad[...] = jnp.zeros_like(dist_grad)
    to_across, to_mate = [], []
    for k, block in enumerate((in_x, in_m, in_g)):
        to_across.append(remote(block.at[1 - x], full.at[k, own], 25 + k, across))
        to_mate.append(remote(block.at[x], full.at[k, own], 28 + k, mate))
        full[k, own] = block[x]

    loads = [
        pltpu.make_async_copy(w_in, w, ssem.at[40]), pltpu.make_async_copy(wd_in, wd, ssem.at[41])]
    for copy in loads:
        copy.start()
    for copy in loads:
        copy.wait()

    def separate(first, second, ref, lanes, rows_at, count):
        def part(i):
            at = tile(i, 128, 128) if rows_at is None else rows_at(i)
            a, b = ref[0, at, lanes].astype(F32), ref[1, at, lanes].astype(F32)
            first(at, jnp.where(low, a, b).astype(BF16))
            second(at, roll_half(jnp.where(low, b, a)).astype(BF16))

        repeat(count, part)

    def store(ref, lead, lanes):
        def put(at, value):
            ref[lead, at, lanes] = value
        return put

    for t in range(12):
        lanes = slice(128 * t, 128 * t + 128)
        inside = slice(128 * (t % 3), 128 * (t % 3) + 128)
        first, second = store(w, 0, lanes), store(w, 1, lanes)
        if t // 3 == 1:
            second = store(w_cq, c, inside)
        if t // 3 == 3:
            first, second = store(w_o, c, inside), store(w_co, c, inside)
        separate(first, second, w, lanes, None, 6)

    halves = []
    for k, ref in enumerate((w_o, w_cq, w_co)):
        halves.append(remote(ref.at[c], ref.at[c], 31 + k, mate))

    for t in range(3):
        lanes = slice(128 * t, 128 * t + 128)

        def part(i):
            at = tile(i, 128, 128)
            a, b = wd[0, at, lanes].astype(F32), wd[1, at, lanes].astype(F32)
            wd[0, at, lanes] = jnp.where(low, a, b).astype(BF16)
            wd[1, at, lanes] = roll_half(jnp.where(low, b, a)).astype(BF16)

        repeat(8, part)
    for xs in range(2):
        for b in range(2):
            piece = wd.at[b, tile((1 - c) + 2 * xs, 256, 256)]
            halves.append(remote(piece, w_d.at[c, 2 * xs + b], 34 + 2 * xs + b, mate))
            w_d[c, 2 * xs + b] = wd[b, tile(c + 2 * xs, 256, 256)]

    gains[...] = w[0, :, 2560:2688].astype(F32).T[0:8]
    hot = (lax.broadcasted_iota(jnp.int32, (BUCKETS, T), 0) == buckets[...]).astype(BF16)
    by_distance = lax.dot_general(pos_bias[...], hot, (((0,), (0,)), ((), ())), preferred_element_type=F32)
    total = lax.broadcasted_iota(jnp.int32, (T, T), 0) + lax.broadcasted_iota(jnp.int32, (T, T), 1)
    mirror = ((total == 0) | (total == T)).astype(BF16)
    work[0:HEADS] = dotf(by_distance.astype(BF16), mirror)
    for t in range(3):
        for a in range(2):
            table[2 * t + a : 2 * t + a + 1] = work[pl.ds(3 * (2 * a + c) + t, 1), :]
    seg_row = segments[pl.ds(x, 1), :]
    seg_col = jnp.broadcast_to(seg_row.astype(F32), (128, T)).T[:, 0:1].astype(jnp.int32)

    for qt in range(2):
        rows = slice(256 * qt, 256 * qt + 256)
        qpos = lax.broadcasted_iota(jnp.int32, (256, T), 0) + 256 * qt
        kpos = lax.broadcasted_iota(jnp.int32, (256, T), 1)
        allowed = (kpos <= qpos) & (seg_col[rows, :] == seg_row)
        work[0:256] = jnp.where(allowed, 0.0, NEG)

        def build(h):
            line = jnp.broadcast_to(table[pl.ds(h, 1), :], (256, T))
            line = pltpu.roll(line, 256 * qt, 1, stride=1, stride_axis=0)
            bias[h, rows] = (line + work[0:256]).astype(BF16)

        repeat(6, build)

    relays = []
    for k in range(3):
        to_across[k].wait_recv()
        relays.append(remote(full.at[k, other], full.at[k, other], k, mate))
    for k in range(3):
        to_mate[k].wait_recv()
        relays[k].wait_recv()

    def order_grad(i):
        chunk = tile(i, 128, 128)
        for n, value in enumerate(sliced_order(lane_tiles(full[2, chunk].astype(F32)))):
            ffb[chunk, 128 * n : 128 * n + 128] = value.astype(BF16)

    repeat(4, order_grad)

    def norm(source, gain, dest):
        def part(i):
            chunk = tile(i, 128, 128)
            v = source(chunk)
            dest[chunk] = (v * rms_scale(v) * gains[gain : gain + 1]).astype(BF16)

        repeat(4, part)

    norm(lambda k: full[0, k].astype(F32), 0, na)

    qkv[:, 0:H] = (dotf(na[...], w[0, :, 0:H]).astype(BF16) * 0.125).astype(BF16)
    qkv[:, H : 2 * H] = dotf(na[...], w[1, :, 0:H]).astype(BF16)
    qkv[:, 2 * H :] = dotf(na[...], w[0, :, H : 2 * H]).astype(BF16)

    def attend(t, q, qo, k, ko, v, vo, bias_ref, probs, out):
        qc, kc, vc = tile(t + qo, 128, 128), tile(t + ko, 128, 128), tile(t + vo, 128, 128)
        oc = tile(t + 3 * c, 128, 128)
        for qt in range(2):
            rows = slice(256 * qt, 256 * qt + 256)
            nk = T if bias_ref is None else 256 * (qt + 1)
            q2, k2, v2 = q[rows, qc], k[0:nk, kc], v[0:nk, vc]
            outs = []
            for a in range(2):
                s = dot_t(jnp.where(masks[a], q2, jnp.zeros_like(q2)), k2)
                if bias_ref is not None:
                    s = s + bias_ref[2 * t + a, rows, 0:nk].astype(F32)
                e = jnp.exp(s - jnp.max(s, axis=-1, keepdims=True))
                prob = (e * (1.0 / jnp.sum(e, axis=-1, keepdims=True))).astype(BF16)
                probs[2 * t + a, rows, 0:nk] = prob
                outs.append(dotf(prob, v2))
            out[rows, oc] = jnp.where(low, outs[0], outs[1]).astype(BF16)

    def attend_back(t, q, qo, k, ko, v, vo, probs, out, causal, gq, gqo, gk, gko, gv, gvo):
        qc, kc, vc = tile(t + qo, 128, 128), tile(t + ko, 128, 128), tile(t + vo, 128, 128)
        oc, gc = tile(t + 3 * c, 128, 128), tile(t, 128, 128)
        qt_s[...] = q[:, qc].T
        gt_s[...] = gatt[:, gc].T
        for qt in (1, 0):
            rows = slice(256 * qt, 256 * qt + 256)
            nk = 256 * (qt + 1) if causal else T
            k2, v2 = k[0:nk, kc], v[0:nk, vc]
            g2 = gatt[rows, gc]
            both = g2.astype(F32) * out[rows, oc].astype(F32)
            outs = []
            for a in range(2):
                half = slice(64 * a, 64 * a + 64)
                delta = jnp.sum(jnp.where(masks[a], both, 0.0), axis=-1, keepdims=True)
                dp = dot_t(jnp.where(masks[a], g2, jnp.zeros_like(g2)), v2)
                prob = probs[2 * t + a, rows, 0:nk]
                ds = (prob.astype(F32) * (dp - delta)).astype(BF16)
                outs.append(dotf(ds, k2))
                dk = dotf(qt_s[half, rows], ds)
                dv = dotf(gt_s[half, rows], prob)
                if qt == 1:
                    dk_t[half, :] = dk
                    dv_t[half, :] = dv
                else:
                    dk_t[half, 0:nk] += dk
                    dv_t[half, 0:nk] += dv
                if causal:
                    band = slice(256 * a, 256 * a + 256)
                    if qt == 1:
                        work[band] = dotf(flip, ds)
                    else:
                        work[band, 256:T] += dotf(flip, ds)
                        turned = pltpu.roll(work[band], 0, 1, stride=1, stride_axis=0)
                        dist_grad[pl.ds(2 * t + a, 1), :] = jnp.sum(turned, axis=0, keepdims=True)
            gq[rows, tile(t + gqo, 128, 128)] = (jnp.where(low, outs[0], outs[1]) * 0.125).astype(BF16)
        gk[:, tile(t + gko, 128, 128)] = dk_t[...].T.astype(BF16)
        gv[:, tile(t + gvo, 128, 128)] = dv_t[...].T.astype(BF16)

    def send_head(ref, t, slot):
        cols = tile(t + 3 * c, 128, 128)
        return remote(ref.at[:, cols], ref.at[:, cols], slot + t, mate)

    def wait_all(copies):
        for copy in copies:
            copy.wait_recv()

    copies = []
    for t in range(3):
        attend(t, qkv, 0, qkv, 3, qkv, 6, bias, p_self, att)
        copies.append(send_head(att, t, 3))

    for k in range(2):
        mkv[:, H * k : H * k + H] = dotf(full[1], w[k, :, 2 * H : 3 * H]).astype(BF16)
    wait_all(halves)
    wait_all(copies)

    def natural_heads(source, dest):
        def part(i):
            chunk = tile(i, 128, 128)
            for n, value in enumerate(natural_order(lane_tiles(source[chunk].astype(F32)))):
                dest[chunk, 128 * n : 128 * n + 128] = value.astype(BF16)

        repeat(4, part)

    def residual(before, heads, weight, dest):
        def part(i):
            chunk = tile(i, 256, 256)
            parts = lane_tiles(dotf(heads[chunk], weight[0])) + lane_tiles(dotf(heads[chunk], weight[1]))
            for n, value in enumerate(natural_order(parts)):
                cols = slice(128 * n, 128 * n + 128)
                dest[chunk, cols] = before(chunk, cols) + value

        repeat(2, part)

    natural_heads(att, attn)
    residual(lambda r, k: full[0, r, k].astype(F32), attn, w_o, x1)
    norm(lambda k: x1[k], 1, nb)
    cq[...] = (dotf(nb[...], w_cq[c]).astype(BF16) * 0.125).astype(BF16)

    copies = []
    for t in range(3):
        attend(t, cq, 0, mkv, 0, mkv, 3, None, p_cross, catt)
        copies.append(send_head(catt, t, 6))
    wait_all(copies)

    natural_heads(catt, cattn)
    residual(lambda r, k: x1[r, k], cattn, w_co, x2)
    norm(lambda k: x2[k], 2, nc)

    def feed(n):
        cols = tile(n, 256, 256)
        xs, b = lax.div(n, 2), lax.rem(n, 2)
        gate = dotf(nc[...], w[xs, :, tile(6 + b, 256, 256)])
        up = dotf(nc[...], w[xs, :, tile(8 + b, 256, 256)])
        back = dot_t(ffb[:, 0:H], w_d[0, n]) + dot_t(ffb[:, H:], w_d[1, n])
        square = gate * gate
        th = jnp.tanh(0.7978845608028654 * gate * (1.0 + 0.044715 * square))
        half = 0.5 * (1.0 + th)
        act = gate * half
        slope = half + 0.5 * gate * (1.0 - th * th) * (0.7978845608028654 * (1.0 + 0.134145 * square))
        hidden[:, cols] = (act * up).astype(BF16)
        gg[:, cols] = (back * up * slope).astype(BF16)
        gu[:, cols] = (back * act).astype(BF16)

    repeat(4, feed)

    gc_copies = []
    for n in range(3):
        cols = slice(256 * n, 256 * n + 256)
        part = dot_t(gg[:, 0:512], w[0, cols, 1536:2048]) + dot_t(gu[:, 0:512], w[0, cols, 2048:2560])
        part = part + dot_t(gg[:, 512:], w[1, cols, 1536:2048]) + dot_t(gu[:, 512:], w[1, cols, 2048:2560])
        gsend[:, cols] = part.astype(BF16)
        gc_copies.append(remote(gsend.at[:, cols], grecv.at[:, cols], 9 + n, mate))

    def pair_partial(product, buf_send, buf_recv, slot):
        def part(n):
            cols = tile(n, 256, 256)
            value = product(cols).astype(BF16)
            for b in range(4):
                buf_send[b, :, cols] = value[128 * b : 128 * b + 128]

        if product is not None:
            repeat(3, part)
        return [remote(buf_send.at[2 * k + (1 - c)], buf_recv.at[k], slot + k, mate) for k in range(2)]

    def down(b):
        chunk = tile(b, 128, 128)
        parts = []
        for p in range(2):
            total = dotf(hidden[chunk, 0:256], w_d[p, 0])
            for n in range(1, 4):
                total = total + dotf(hidden[chunk, 256 * n : 256 * n + 256], w_d[p, n])
            parts = parts + lane_tiles(total)
        for n, value in enumerate(natural_order(parts)):
            psend[0, b, :, 128 * n : 128 * n + 128] = value.astype(BF16)

    repeat(4, down)
    mix_copies = pair_partial(None, psend.at[0], precv.at[0], 12)

    def weight_grad(left, left_rows, grads):
        def turn(j):
            left_t[tile(j, 128, 128), :] = left(tile(j, 128, 128)).T

        repeat(left_rows // 128, turn)
        for grad, dest, count in grads:
            def part(n):
                dest(n, dotf(left_t[0:left_rows], grad(n)))

            repeat(count, part)

    def into(lead_of, first):
        def put(n, value):
            gw[lead_of(n), :, tile(first(n), 128, 128)] = value.astype(BF16)
        return put

    def pack_first(value, a, b):
        return jnp.where(low, value, a.astype(F32)).astype(BF16), jnp.where(low, b.astype(F32), value).astype(BF16)

    def pack_second(value, a, b):
        value = roll_half(value)
        return jnp.where(low, a.astype(F32), value).astype(BF16), jnp.where(low, value, b.astype(F32)).astype(BF16)

    def into_pair(group, pack):
        def put(n, value):
            cols = tile(n + 3 * group, 128, 128)
            gw[0, :, cols], gw[1, :, cols] = pack(value, gw[0, :, cols], gw[1, :, cols])
        return put

    def cols_of(ref, first=0):
        return lambda n: ref[:, tile(n + first, 128, 128)]

    weight_grad(lambda j: nc[:, j], D, [
        (cols_of(gg), into(lambda n: lax.div(n, 4), lambda n: 12 + lax.rem(n, 4)), 8),
        (cols_of(gu), into(lambda n: lax.div(n, 4), lambda n: 16 + lax.rem(n, 4)), 8),
    ])

    def put_down(half):
        def put(n, value):
            cols = tile(n, 128, 128)
            for xs in range(2):
                top = value[512 * xs : 512 * xs + 256]
                bottom = roll_half(value[512 * xs + 256 : 512 * xs + 512])
                a, b = jnp.where(low, top, bottom).astype(BF16), jnp.where(low, bottom, top).astype(BF16)
                if half:
                    rows = tile(c + 2 * xs, 256, 256)
                    gwd[0, rows, cols] = a
                    gwd[1, rows, cols] = b
                else:
                    gdsend[xs, 0, :, cols] = a
                    gdsend[xs, 1, :, cols] = b
        return put

    weight_grad(lambda j: hidden[:, j], FH, [
        (lambda n: ffb[:, tile(n + 3 * (1 - c), 128, 128)], put_down(False), 3),
        (lambda n: ffb[:, tile(n + 3 * c, 128, 128)], put_down(True), 3),
    ])
    gd_copies = [
        remote(gdsend.at[xs], gwd.at[:, tile(c + 2 * xs, 256, 256)], 38 + xs, mate) for xs in range(2)
    ]

    wait_all(gc_copies)
    small[...] = jnp.zeros_like(small)

    def keep_gain(index, i, gain):
        small[index : index + 1, 0:D] += jnp.where(lax.rem(i, 2) == c, gain, 0.0)

    def keep_sliced(chunk, total):
        for n, value in enumerate(sliced_order(lane_tiles(total))):
            gxb[chunk, 128 * n : 128 * n + 128] = value.astype(BF16)

    def back_heads(weight):
        for t in range(3):
            first, second = tile(3 * c + t, 64, 64), tile(3 * c + t + 6, 64, 64)
            part = None
            for p in range(2):
                rows = jnp.concatenate([weight[p, first], weight[p, second]], axis=0)
                term = dot_t(gxb[:, H * p : H * p + H], rows)
                part = term if part is None else part + term
            gatt[:, 128 * t : 128 * t + 128] = part.astype(BF16)

    def third(i):
        chunk = tile(i, 128, 128)
        upstream = gsend[chunk].astype(F32) + grecv[chunk].astype(F32)
        gv, gain = norm_back(x2[chunk], gains[2:3], upstream)
        total = full[2, chunk].astype(F32) + gv
        gx2[chunk] = total
        keep_sliced(chunk, total)
        keep_gain(2, i, gain)

    repeat(4, third)
    back_heads(w_co)
    gmkv = grecv
    copies = []
    for t in range(3):
        attend_back(t, cq, 0, mkv, 0, mkv, 3, p_cross, catt, False, gcq, 3 * c, gmkv, 0, gmkv, 3)
        copies.append(send_head(gcq, t, 14))

    mem_copies = pair_partial(lambda k: dot_t(gmkv[:, 0:H], w[0, k, 2 * H : 3 * H]) + dot_t(gmkv[:, H:], w[1, k, 2 * H : 3 * H]), psend.at[1], precv.at[1], 17)

    wait_all(mix_copies)

    def mixed_block(k, chunk):
        return (x2[chunk] + psend[0, 2 * k + c].astype(F32) + precv[0, k].astype(F32)).astype(BF16)

    msend[0] = mixed_block(1 - x, other)
    mix_out = remote(msend.at[0], mixed.at[x], 19, across)
    mixed[x] = mixed_block(x, own)

    weight_grad(lambda j: cattn[:, j], D, [(cols_of(gxb, 3 * c), into_pair(3, pack_second), 3)])
    wait_all(copies)

    def back_b(n):
        cols = tile(n, 256, 256)
        x2[:, cols] = dot_t(gcq[:, 0:H], w_cq[0, cols]) + dot_t(gcq[:, H:], w_cq[1, cols])

    repeat(3, back_b)

    def second(i):
        chunk = tile(i, 128, 128)
        gv, gain = norm_back(x1[chunk], gains[1:2], x2[chunk])
        total = gx2[chunk] + gv
        gx2[chunk] = total
        keep_sliced(chunk, total)
        keep_gain(1, i, gain)

    repeat(4, second)
    back_heads(w_o)
    for t in range(3):
        attend_back(t, qkv, 0, qkv, 3, qkv, 6, p_self, att, True, gg, 0, gg, 3, gu, 0)

    def back_a(k):
        part = dot_t(gg[:, 0:H], w[0, k, 0:H]) + dot_t(gg[:, H : 2 * H], w[1, k, 0:H])
        return part + dot_t(gu[:, 0:H], w[0, k, H : 2 * H])

    ig_copies = pair_partial(back_a, psend.at[2], precv.at[2], 21)

    weight_grad(lambda j: full[1, :, j], D, [
        (cols_of(gmkv), into_pair(2, pack_first), 3), (cols_of(gmkv, 3), into_pair(2, pack_second), 3)])
    norm(lambda k: x1[k], 1, nb)
    weight_grad(lambda j: nb[:, j], D, [(cols_of(gcq, 3 * c), into_pair(1, pack_second), 3)])
    weight_grad(lambda j: attn[:, j], D, [(cols_of(gxb, 3 * c), into_pair(3, pack_first), 3)])
    norm(lambda k: full[0, k].astype(F32), 0, na)
    weight_grad(lambda j: na[:, j], D, [
        (cols_of(gg), into_pair(0, pack_first), 3), (cols_of(gg, 3), into_pair(0, pack_second), 3),
        (cols_of(gu), into_pair(1, pack_first), 3)])

    flipped = (
        lax.broadcasted_iota(jnp.int32, (T, T), 0) + lax.broadcasted_iota(jnp.int32, (T, T), 1) == T - 1
    ).astype(F32)
    by_bucket = (
        jnp.broadcast_to(buckets[...], (128, T)) == lax.broadcasted_iota(jnp.int32, (128, T), 0)
    ).astype(F32)
    high = lax.Precision.HIGHEST
    distances = jnp.dot(dist_grad[...], flipped, precision=high, preferred_element_type=F32)
    per_head = lax.dot_general(
        distances, by_bucket, (((1,), (1,)), ((), ())), precision=high, preferred_element_type=F32)
    for t in range(3):
        for a in range(2):
            here = lax.broadcasted_iota(jnp.int32, (16, 128), 0) == 3 * (2 * a + c) + t
            small[:, D:] += jnp.where(here, per_head[2 * t + a : 2 * t + a + 1], 0.0)

    wait_all(mem_copies)
    msend[1] = (psend[1, 2 * (1 - x) + c].astype(F32) + precv[1, 1 - x].astype(F32)).astype(BF16)
    mem_out = remote(msend.at[1], late.at[0], 20, across)
    memory_grad[x] = psend[1, 2 * x + c].astype(F32) + precv[1, x].astype(F32)

    wait_all(ig_copies)

    def first_block(k, chunk):
        upstream = psend[2, 2 * k + c].astype(F32) + precv[2, k].astype(F32)
        gv, gain = norm_back(full[0, chunk].astype(F32), gains[0:1], upstream)
        small[0:1, 0:D] += gain
        return gx2[chunk] + gv

    msend[2] = first_block(1 - x, other).astype(BF16)
    ig_out = remote(msend.at[2], late.at[1], 23, across)
    input_grad[x] = first_block(x, own)

    mem_out.wait_recv()
    memory_grad[1 - x] = late[0].astype(F32)
    ig_out.wait_recv()
    input_grad[1 - x] = late[1].astype(F32)
    mix_out.wait_recv()
    wait_all(gd_copies)
    for copy in started:
        copy.wait_send()


def layer(blocks, segments, buckets, pos_bias, w, wd):
    def bf(*shape):
        return VMEM(shape, BF16)

    def fl(*shape):
        return VMEM(shape, F32)

    outs = [
        ((2, 128, D), BF16), ((2, 128, D), F32), ((2, 128, D), F32), ((16, D + 128), F32),
        ((2, D, 2560), BF16), ((2, FH, H), BF16),
    ]
    whole = pl.BlockSpec(memory_space=pltpu.VMEM)
    return pl.pallas_call(
        layer_kernel,
        out_shape=[jax.ShapeDtypeStruct(s, d) for s, d in outs],
        in_specs=[whole] * 6 + [pl.BlockSpec(memory_space=pl.ANY)] * 2,
        out_specs=[whole] * len(outs),
        scratch_shapes=[
            bf(2, D, 2688), bf(2, FH, H),
            bf(2, D, H), bf(2, D, H), bf(2, D, H), bf(2, 4, 256, H), fl(8, D), fl(8, T), fl(8, T),
            bf(3, T, D), bf(T, D), bf(T, D), bf(T, 3 * H), bf(T, D), bf(T, D), fl(T, D),
            bf(T, H), bf(T, D), bf(T, D), bf(T, D), fl(T, D),
            bf(6, T, T), bf(6, T, T), bf(T, FH), bf(T, FH), bf(T, FH), bf(T, D), bf(T, D),
            fl(T, D), bf(T, D),
            bf(T, D), fl(128, T), fl(128, T), bf(128, T), bf(128, T),
            bf(FH, T), fl(T, T),
            bf(3, 4, 128, D), bf(3, 2, 128, D), bf(3, 128, D), bf(2, 128, D), bf(2, 2, 256, H),
            pltpu.SemaphoreType.DMA((42,)), pltpu.SemaphoreType.DMA((40,)),
        ],
        input_output_aliases={},
        compiler_params=pltpu.CompilerParams(
            collective_id=0, has_side_effects=True, vmem_limit_bytes=67043328),
        name="layer",
    )(*blocks, segments, buckets.reshape(1, T), pos_bias, w, wd)


PAIRS = ((0, 1), (2, 4), (5, 6), (3, 7))


def pack_pair(a, b, x):
    n = a.shape[0]
    both = jnp.stack([a.reshape(n, 3, 64), b.reshape(n, 3, 64)], axis=2)
    return jnp.where(x == 0, both, both[:, :, ::-1]).reshape(n, H)


def unpack_pair(v, x):
    both = v.reshape(v.shape[0], 3, 2, 64)
    both = jnp.where(x == 0, both, both[:, :, ::-1])
    return both[:, :, 0].reshape(-1, 192), both[:, :, 1].reshape(-1, 192)


def hidden_order(v, half, forward=True):
    n = v.shape[0]
    outer = v.shape[1] // (2 * half)
    v = v.reshape((n, outer, 2, half) if forward else (n, 2, outer, half))
    return v.transpose(0, 2, 1, 3).reshape(n, -1)


def gather_plain(squares, gate, up, down, gains, x):
    half = down.shape[0] // 2
    parts = [pack_pair(squares[a], squares[b], x) for a, b in PAIRS]
    parts += [hidden_order(gate, half), hidden_order(up, half)]
    parts.append(jnp.pad(gains.T, ((0, 0), (0, 125))))
    groups = [[0, 2], [1, 3]]

    def both(v):
        v = lax.all_gather(v, "rows", axis=0, tiled=True)
        return lax.all_gather(v, "seq", axis=0, axis_index_groups=groups)

    return both(jnp.concatenate(parts, axis=1)), both(pack_pair(down[:half], down[half:], x))


def scatter_plain(gw, gwd, small, x):
    def reduced(v):
        v = lax.psum_scatter(v, "rows", scatter_dimension=1, tiled=True)
        kept = lax.dynamic_index_in_dim(v, x, 0, keepdims=False).astype(F32)
        sent = lax.dynamic_index_in_dim(v, 1 - x, 0, keepdims=False)
        return kept + lax.ppermute(sent, "seq", [(0, 2), (2, 0), (1, 3), (3, 1)]).astype(F32)

    total, down = reduced(gw), reduced(gwd)
    half = down.shape[0]
    squares = [None] * 8
    for k, (a, b) in enumerate(PAIRS):
        squares[a], squares[b] = unpack_pair(total[:, H * k : H * k + H], x)
    gate = hidden_order(total[:, 1536:2048], half, False)
    up = hidden_order(total[:, 2048:], half, False)
    down = jnp.concatenate(unpack_pair(down, x), axis=0)
    return squares, gate, up, down, lax.psum(small, ("rows", "seq"))


def shards(
    layer_input, memory, output_grad, segments, buckets,
    self_query, self_key, self_value, self_output,
    cross_query, cross_key, cross_value, cross_output,
    gate_weight, up_weight, down_weight, norm_gains, position_bias,
):
    x = lax.axis_index("seq") // 2
    squares = (self_query, self_key, self_value, self_output, cross_query, cross_key, cross_value, cross_output)
    w, wd = gather_plain(squares, gate_weight, up_weight, down_weight, norm_gains, x)
    mixed, input_grad, memory_grad, small, gw, gwd = layer(
        (layer_input, memory, output_grad), segments, buckets, position_bias, w, wd)
    squares, gate, up, down, small = scatter_plain(gw, gwd, small, x)
    width = D // lax.axis_size("rows")
    gains = lax.dynamic_slice(small, (0, lax.axis_index("rows") * width), (3, width))
    return (mixed, input_grad, memory_grad, *squares, gate, up, down, gains, small[:HEADS, D : D + BUCKETS].T)


def solution(mesh):
    tokens = P("rows", "seq", None)
    weight = P("rows", "seq")
    return jax.shard_map(
        shards,
        mesh=mesh,
        in_specs=(tokens, tokens, tokens, P("rows", None), P()) + (weight,) * 11 + (P(None, "rows"), P()),
        out_specs=(tokens,) * 3 + (weight,) * 11 + (P(None, "rows"), P()),
        check_vma=False,
    )
```

```python
import functools

import jax
import jax.numpy as jnp
from jax import lax
from jax.experimental import pallas as pl
from jax.experimental.pallas import tpu as pltpu
from jax.sharding import PartitionSpec as P

HEADS = 12
BUCKETS = 32
EPS = 1e-06
NEG = -1e30
F32 = jnp.float32
BF16 = jnp.bfloat16
MESH = pl.DeviceIdType.MESH
T = 512
D = 768
H = 384
FH = 1024
VMEM = pltpu.VMEM


def dotf(a, b):
    return jnp.dot(a, b, preferred_element_type=F32)


def dot_t(a, b):
    return lax.dot_general(a, b, (((1,), (1,)), ((), ())), preferred_element_type=F32)


def repeat(count, body):
    lax.fori_loop(0, count, lambda i, carry: (body(i), carry)[1], 0)


def tile(start, step, size):
    return pl.ds(pl.multiple_of(start * step, step), size)


def rms_scale(v):
    return lax.rsqrt(jnp.mean(v * v, axis=-1, keepdims=True) + EPS)


def norm_back(v, gain, upstream):
    r = rms_scale(v)
    scaled = gain * upstream
    gv = r * scaled - v * (r * r * r) * jnp.mean(scaled * v, axis=-1, keepdims=True)
    return gv, jnp.sum(upstream * v * r, axis=0, keepdims=True)


def roll_half(v):
    return pltpu.roll(v, 64, 1)


def low_lanes():
    return lax.broadcasted_iota(jnp.int32, (1, 128), 1) < 64


def sliced_order(tiles):
    low = low_lanes()
    out = []
    for n in range(6):
        a, b = tiles[n // 2], tiles[n // 2 + 3]
        out.append(jnp.where(low, a, roll_half(b)) if n % 2 == 0 else jnp.where(low, roll_half(a), b))
    return out


def natural_order(tiles):
    low = low_lanes()
    out = [jnp.where(low, tiles[2 * k], roll_half(tiles[2 * k + 1])) for k in range(3)]
    return out + [jnp.where(low, roll_half(tiles[2 * k]), tiles[2 * k + 1]) for k in range(3)]


def lane_tiles(v):
    return [v[:, 128 * n : 128 * n + 128] for n in range(v.shape[1] // 128)]


GATHER = (
    ("w", 2560, 128, 0), ("w", 0, H, 0), ("w", H, H, 1), ("w", 2 * H, H, 0), ("w", 3 * H, H, 1),
    ("w", 1536, 512, 0), ("w", 2048, 512, 1), ("d", 0, 64, 0), ("d", 64, 64, 1),
)
SCATTER = (
    ("w", 1536, 512, 0), ("w", 2048, 512, 1), ("d", 0, 64, 0), ("d", 64, 64, 1),
    ("w", 2 * H, H, 0), ("w", 3 * H, H, 1), ("w", 0, H, 0), ("w", H, H, 1),
)


def place():
    row, seq = lax.axis_index("rows"), lax.axis_index("seq")
    return lax.div(row, 2), lax.rem(row, 2), lax.div(seq, 2), lax.rem(seq, 2)


def device(z, y, x, c):
    return (2 * z + y, 2 * x + c)


class Gather:
    def __init__(self, own_w, own_d, w, wd, ssem, rsem):
        self.refs = (own_w, own_d, w, wd, ssem, rsem)
        self.z, self.y, self.x, self.c = place()
        self.sent = []
        self.open = {}
        self.todo = []
        count = len(GATHER)
        for k in range(min(3, count)):
            self.todo.append((self.begin, k))
        for k in range(count):
            self.todo.append((self.after_z, k))
            if k + 3 < count:
                self.todo.append((self.begin, k + 3))
            if k >= 1:
                self.todo.append((self.after_p, k - 1))
            if k >= 2:
                self.todo.append((self.finish, k - 2))
        self.todo += [(self.after_p, count - 1), (self.finish, count - 2), (self.finish, count - 1)]
        self.done = -1

    def view(self, k, x, z, y):
        kind, first, size, _ = GATHER[k]
        _, _, w, wd, _, _ = self.refs
        r = 2 * z + y
        if kind == "w":
            return w.at[x, pl.ds(pl.multiple_of(96 * r, 96), 96), first : first + size]
        return wd.at[x, pl.ds(pl.multiple_of(128 * r + first, 64), size), :]

    def own(self, k):
        kind, first, size, _ = GATHER[k]
        own_w, own_d, _, _, _, _ = self.refs
        return own_w.at[:, first : first + size] if kind == "w" else own_d.at[first : first + size, :]

    def peers(self, k):
        y_peer, x_peer = device(self.z, 1 - self.y, self.x, self.c), device(self.z, self.y, 1 - self.x, self.c)
        return (x_peer, y_peer) if GATHER[k][3] else (y_peer, x_peer)

    def across_p(self, k):
        return (1 - self.x, self.y) if GATHER[k][3] else (self.x, 1 - self.y)

    def copy(self, k, slot, src, dst, peer):
        _, _, _, _, ssem, rsem = self.refs
        return pltpu.make_async_remote_copy(
            src_ref=src, dst_ref=dst, send_sem=ssem.at[k, slot], recv_sem=rsem.at[k, slot],
            device_id=peer, device_id_type=MESH)

    def send(self, k, *args):
        copy = self.copy(k, *args)
        copy.start()
        self.open[k].append(copy)

    def behind(self, j):
        return lax.rem(self.z + 4 - j, 4)

    def begin(self, k):
        here = self.view(k, self.x, self.z, self.y)
        p, q = self.peers(k)
        own = self.own(k)
        self.open[k] = []
        self.send(k, 3, own, here, p)
        self.send(k, 7, own, here, q)
        for j in range(1, 4):
            self.send(k, j - 1, own, here, device(lax.rem(self.z + j, 4), self.y, self.x, self.c))
        here[...] = own[...]

    def after_z(self, k):
        p, q = self.peers(k)
        for j in range(1, 4):
            block = self.view(k, self.x, self.behind(j), self.y)
            self.copy(k, j - 1, block, block, p).wait_recv()
            self.send(k, 3 + j, block, block, p)
            self.send(k, 7 + j, block, block, q)

    def after_p(self, k):
        p, q = self.peers(k)
        x, y = self.across_p(k)
        for j in range(4):
            block = self.view(k, x, self.behind(j), y)
            self.copy(k, 3 + j, block, block, p).wait_recv()
            self.send(k, 11 + j, block, block, q)

    def finish(self, k):
        p, q = self.peers(k)
        x, y = (self.x, 1 - self.y) if GATHER[k][3] else (1 - self.x, self.y)
        for j in range(4):
            block = self.view(k, x, self.behind(j), y)
            self.copy(k, 7 + j, block, block, q).wait_recv()
        for j in range(4):
            block = self.view(k, 1 - self.x, self.behind(j), 1 - self.y)
            self.copy(k, 11 + j, block, block, q).wait_recv()
        for copy in self.open[k]:
            copy.wait_send()
        self.done = k

    def pump(self, count):
        for _ in range(min(count, len(self.todo))):
            action, k = self.todo.pop(0)
            action(k)

    def need(self, k):
        while self.done < k:
            self.pump(1)


class Loaded:
    def __init__(self, w_in, wd_in, w, wd, sems):
        self.copies = [pltpu.make_async_copy(w_in, w, sems.at[0]), pltpu.make_async_copy(wd_in, wd, sems.at[1])]
        for copy in self.copies:
            copy.start()
        self.sent = []

    def pump(self, count):
        pass

    def need(self, k):
        for copy in self.copies:
            copy.wait()
        self.copies = []


def layer_kernel(
    inside, in_x, in_m, in_g, segments, buckets, pos_bias, w_in, wd_in,
    mixed, input_grad, memory_grad, small, w, wd,
    w_o, w_cq, w_co, w_d, gains, table, dist_grad, full, ffb, na, qkv, att, attn, x1, cq, mkv, catt, cattn, x2,
    bias, p_self, hidden, gg, gu, gsend, grecv, gx2, gxb,
    gcq, dk_t, dv_t, qt_s, gt_s, left_t, work,
    psend, precv, msend, late, gdsend,
    ssem, rsem, gather_ssem, gather_rsem,
):
    p_cross = bias
    gw, gwd = w, wd
    nb = nc = na
    gatt = hidden
    row = lax.axis_index("rows")
    seq = lax.axis_index("seq")
    x = lax.div(seq, 2)
    c = lax.rem(seq, 2)
    mate = (row, 2 * x + (1 - c))
    across = (row, lax.rem(seq + 2, 4))

    barrier = pltpu.get_barrier_semaphore()
    peers = [mate, across]
    if inside:
        pz, py, px, pc = place()
        peers.append(device(pz, 1 - py, px, pc))
        peers += [device(lax.rem(pz + j, 4), py, px, pc) for j in range(1, 4)]
    for peer in peers:
        pl.semaphore_signal(barrier, inc=1, device_id=peer, device_id_type=MESH)
    pl.semaphore_wait(barrier, len(peers))

    started = []

    def remote(src, dst, slot, peer, keep=True):
        copy = pltpu.make_async_remote_copy(
            src_ref=src, dst_ref=dst, send_sem=ssem.at[slot], recv_sem=rsem.at[slot],
            device_id=peer, device_id_type=MESH)
        copy.start()
        if keep:
            started.append(copy)
        return copy

    mine = tile(c, H, H)
    low = lax.broadcasted_iota(jnp.int32, (1, 128), 1) < 64
    masks = (low, jnp.logical_not(low))
    flip = (
        lax.broadcasted_iota(jnp.int32, (256, 256), 0)
        + lax.broadcasted_iota(jnp.int32, (256, 256), 1)
        == 255
    ).astype(BF16)

    own = tile(seq, 128, 128)
    other = tile(lax.rem(seq + 2, 4), 128, 128)
    dist_grad[...] = jnp.zeros_like(dist_grad)
    to_across, to_mate = [], []
    for k, block in enumerate((in_x, in_m, in_g)):
        to_across.append(remote(block.at[1 - x], full.at[k, own], 25 + k, across))
        to_mate.append(remote(block.at[x], full.at[k, own], 28 + k, mate))
        full[k, own] = block[x]

    if inside:
        weights = Gather(w_in, wd_in, w, wd, gather_ssem, gather_rsem)
    else:
        weights = Loaded(w_in, wd_in, w, wd, gather_ssem)
    weights.need(8)

    def separate(first, second, ref, lanes, rows_at, count):
        def part(i):
            at = tile(i, 128, 128) if rows_at is None else rows_at(i)
            a, b = ref[0, at, lanes].astype(F32), ref[1, at, lanes].astype(F32)
            first(at, jnp.where(low, a, b).astype(BF16))
            second(at, roll_half(jnp.where(low, b, a)).astype(BF16))

        repeat(count, part)

    def store(ref, lead, lanes):
        def put(at, value):
            ref[lead, at, lanes] = value
        return put

    for t in range(12):
        lanes = slice(128 * t, 128 * t + 128)
        inside = slice(128 * (t % 3), 128 * (t % 3) + 128)
        first, second = store(w, 0, lanes), store(w, 1, lanes)
        if t // 3 == 1:
            second = store(w_cq, c, inside)
        if t // 3 == 3:
            first, second = store(w_o, c, inside), store(w_co, c, inside)
        separate(first, second, w, lanes, None, 6)

    halves = []
    for k, ref in enumerate((w_o, w_cq, w_co)):
        halves.append(remote(ref.at[c], ref.at[c], 31 + k, mate, False))

    for t in range(3):
        lanes = slice(128 * t, 128 * t + 128)

        def part(i):
            at = tile(i, 128, 128)
            a, b = wd[0, at, lanes].astype(F32), wd[1, at, lanes].astype(F32)
            wd[0, at, lanes] = jnp.where(low, a, b).astype(BF16)
            wd[1, at, lanes] = roll_half(jnp.where(low, b, a)).astype(BF16)

        repeat(8, part)
    for xs in range(2):
        for b in range(2):
            piece = wd.at[b, tile((1 - c) + 2 * xs, 256, 256)]
            halves.append(remote(piece, w_d.at[c, 2 * xs + b], 34 + 2 * xs + b, mate, False))
            w_d[c, 2 * xs + b] = wd[b, tile(c + 2 * xs, 256, 256)]

    for copy in halves:
        copy.wait_send()

    gains[...] = w[0, :, 2560:2688].astype(F32).T[0:8]
    hot = (lax.broadcasted_iota(jnp.int32, (BUCKETS, T), 0) == buckets[...]).astype(BF16)
    by_distance = lax.dot_general(pos_bias[...], hot, (((0,), (0,)), ((), ())), preferred_element_type=F32)
    total = lax.broadcasted_iota(jnp.int32, (T, T), 0) + lax.broadcasted_iota(jnp.int32, (T, T), 1)
    mirror = ((total == 0) | (total == T)).astype(BF16)
    work[0:HEADS] = dotf(by_distance.astype(BF16), mirror)
    for t in range(3):
        for a in range(2):
            table[2 * t + a : 2 * t + a + 1] = work[pl.ds(3 * (2 * a + c) + t, 1), :]
    seg_row = segments[pl.ds(x, 1), :]
    seg_col = jnp.broadcast_to(seg_row.astype(F32), (128, T)).T[:, 0:1].astype(jnp.int32)

    for qt in range(2):
        rows = slice(256 * qt, 256 * qt + 256)
        qpos = lax.broadcasted_iota(jnp.int32, (256, T), 0) + 256 * qt
        kpos = lax.broadcasted_iota(jnp.int32, (256, T), 1)
        allowed = (kpos <= qpos) & (seg_col[rows, :] == seg_row)
        work[0:256] = jnp.where(allowed, 0.0, NEG)

        def build(h):
            line = jnp.broadcast_to(table[pl.ds(h, 1), :], (256, T))
            line = pltpu.roll(line, 256 * qt, 1, stride=1, stride_axis=0)
            bias[h, rows] = (line + work[0:256]).astype(BF16)

        repeat(6, build)

    relays = []
    for k in range(3):
        to_across[k].wait_recv()
        relays.append(remote(full.at[k, other], full.at[k, other], k, mate))
    for k in range(3):
        to_mate[k].wait_recv()
        relays[k].wait_recv()

    def order_grad(i):
        chunk = tile(i, 128, 128)
        for n, value in enumerate(sliced_order(lane_tiles(full[2, chunk].astype(F32)))):
            ffb[chunk, 128 * n : 128 * n + 128] = value.astype(BF16)

    repeat(4, order_grad)

    def norm(source, gain, dest):
        def part(i):
            chunk = tile(i, 128, 128)
            v = source(chunk)
            dest[chunk] = (v * rms_scale(v) * gains[gain : gain + 1]).astype(BF16)

        repeat(4, part)

    norm(lambda k: full[0, k].astype(F32), 0, na)

    qkv[:, 0:H] = (dotf(na[...], w[0, :, 0:H]).astype(BF16) * 0.125).astype(BF16)
    qkv[:, H : 2 * H] = dotf(na[...], w[1, :, 0:H]).astype(BF16)
    qkv[:, 2 * H :] = dotf(na[...], w[0, :, H : 2 * H]).astype(BF16)

    def attend(t, q, qo, k, ko, v, vo, bias_ref, probs, out):
        qc, kc, vc = tile(t + qo, 128, 128), tile(t + ko, 128, 128), tile(t + vo, 128, 128)
        oc = tile(t + 3 * c, 128, 128)
        for qt in range(2):
            rows = slice(256 * qt, 256 * qt + 256)
            nk = T if bias_ref is None else 256 * (qt + 1)
            q2, k2, v2 = q[rows, qc], k[0:nk, kc], v[0:nk, vc]
            outs = []
            for a in range(2):
                s = dot_t(jnp.where(masks[a], q2, jnp.zeros_like(q2)), k2)
                if bias_ref is not None:
                    s = s + bias_ref[2 * t + a, rows, 0:nk].astype(F32)
                e = jnp.exp(s - jnp.max(s, axis=-1, keepdims=True))
                prob = (e * (1.0 / jnp.sum(e, axis=-1, keepdims=True))).astype(BF16)
                probs[2 * t + a, rows, 0:nk] = prob
                outs.append(dotf(prob, v2))
            out[rows, oc] = jnp.where(low, outs[0], outs[1]).astype(BF16)

    def attend_back(t, q, qo, k, ko, v, vo, probs, out, causal, gq, gqo, gk, gko, gv, gvo):
        qc, kc, vc = tile(t + qo, 128, 128), tile(t + ko, 128, 128), tile(t + vo, 128, 128)
        oc, gc = tile(t + 3 * c, 128, 128), tile(t, 128, 128)
        qt_s[...] = q[:, qc].T
        gt_s[...] = gatt[:, gc].T
        for qt in (1, 0):
            rows = slice(256 * qt, 256 * qt + 256)
            nk = 256 * (qt + 1) if causal else T
            k2, v2 = k[0:nk, kc], v[0:nk, vc]
            g2 = gatt[rows, gc]
            both = g2.astype(F32) * out[rows, oc].astype(F32)
            outs = []
            for a in range(2):
                half = slice(64 * a, 64 * a + 64)
                delta = jnp.sum(jnp.where(masks[a], both, 0.0), axis=-1, keepdims=True)
                dp = dot_t(jnp.where(masks[a], g2, jnp.zeros_like(g2)), v2)
                prob = probs[2 * t + a, rows, 0:nk]
                ds = (prob.astype(F32) * (dp - delta)).astype(BF16)
                outs.append(dotf(ds, k2))
                dk = dotf(qt_s[half, rows], ds)
                dv = dotf(gt_s[half, rows], prob)
                if qt == 1:
                    dk_t[half, :] = dk
                    dv_t[half, :] = dv
                else:
                    dk_t[half, 0:nk] += dk
                    dv_t[half, 0:nk] += dv
                if causal:
                    band = slice(256 * a, 256 * a + 256)
                    if qt == 1:
                        work[band] = dotf(flip, ds)
                    else:
                        work[band, 256:T] += dotf(flip, ds)
                        turned = pltpu.roll(work[band], 0, 1, stride=1, stride_axis=0)
                        dist_grad[pl.ds(2 * t + a, 1), :] = jnp.sum(turned, axis=0, keepdims=True)
            gq[rows, tile(t + gqo, 128, 128)] = (jnp.where(low, outs[0], outs[1]) * 0.125).astype(BF16)
        gk[:, tile(t + gko, 128, 128)] = dk_t[...].T.astype(BF16)
        gv[:, tile(t + gvo, 128, 128)] = dv_t[...].T.astype(BF16)

    def send_head(ref, t, slot):
        cols = tile(t + 3 * c, 128, 128)
        return remote(ref.at[:, cols], ref.at[:, cols], slot + t, mate)

    def wait_all(copies):
        for copy in copies:
            copy.wait_recv()

    copies = []
    for t in range(3):
        attend(t, qkv, 0, qkv, 3, qkv, 6, bias, p_self, att)
        copies.append(send_head(att, t, 3))

    for k in range(2):
        mkv[:, H * k : H * k + H] = dotf(full[1], w[k, :, 2 * H : 3 * H]).astype(BF16)
    wait_all(halves)
    wait_all(copies)

    def natural_heads(source, dest):
        def part(i):
            chunk = tile(i, 128, 128)
            for n, value in enumerate(natural_order(lane_tiles(source[chunk].astype(F32)))):
                dest[chunk, 128 * n : 128 * n + 128] = value.astype(BF16)

        repeat(4, part)

    def residual(before, heads, weight, dest):
        def part(i):
            chunk = tile(i, 256, 256)
            parts = lane_tiles(dotf(heads[chunk], weight[0])) + lane_tiles(dotf(heads[chunk], weight[1]))
            for n, value in enumerate(natural_order(parts)):
                cols = slice(128 * n, 128 * n + 128)
                dest[chunk, cols] = before(chunk, cols) + value

        repeat(2, part)

    natural_heads(att, attn)
    residual(lambda r, k: full[0, r, k].astype(F32), attn, w_o, x1)
    norm(lambda k: x1[k], 1, nb)
    cq[...] = (dotf(nb[...], w_cq[c]).astype(BF16) * 0.125).astype(BF16)

    copies = []
    for t in range(3):
        attend(t, cq, 0, mkv, 0, mkv, 3, None, p_cross, catt)
        copies.append(send_head(catt, t, 6))
    wait_all(copies)

    natural_heads(catt, cattn)
    residual(lambda r, k: x1[r, k], cattn, w_co, x2)
    norm(lambda k: x2[k], 2, nc)

    def feed(n):
        cols = tile(n, 256, 256)
        xs, b = lax.div(n, 2), lax.rem(n, 2)
        gate = dotf(nc[...], w[xs, :, tile(6 + b, 256, 256)])
        up = dotf(nc[...], w[xs, :, tile(8 + b, 256, 256)])
        back = dot_t(ffb[:, 0:H], w_d[0, n]) + dot_t(ffb[:, H:], w_d[1, n])
        square = gate * gate
        th = jnp.tanh(0.7978845608028654 * gate * (1.0 + 0.044715 * square))
        half = 0.5 * (1.0 + th)
        act = gate * half
        slope = half + 0.5 * gate * (1.0 - th * th) * (0.7978845608028654 * (1.0 + 0.134145 * square))
        hidden[:, cols] = (act * up).astype(BF16)
        gg[:, cols] = (back * up * slope).astype(BF16)
        gu[:, cols] = (back * act).astype(BF16)

    repeat(4, feed)

    gc_copies = []
    for n in range(3):
        cols = slice(256 * n, 256 * n + 256)
        part = dot_t(gg[:, 0:512], w[0, cols, 1536:2048]) + dot_t(gu[:, 0:512], w[0, cols, 2048:2560])
        part = part + dot_t(gg[:, 512:], w[1, cols, 1536:2048]) + dot_t(gu[:, 512:], w[1, cols, 2048:2560])
        gsend[:, cols] = part.astype(BF16)
        gc_copies.append(remote(gsend.at[:, cols], grecv.at[:, cols], 9 + n, mate))

    def pair_partial(product, buf_send, buf_recv, slot):
        def part(n):
            cols = tile(n, 256, 256)
            value = product(cols).astype(BF16)
            for b in range(4):
                buf_send[b, :, cols] = value[128 * b : 128 * b + 128]

        if product is not None:
            repeat(3, part)
        return [remote(buf_send.at[2 * k + (1 - c)], buf_recv.at[k], slot + k, mate) for k in range(2)]

    def down(b):
        chunk = tile(b, 128, 128)
        parts = []
        for p in range(2):
            total = dotf(hidden[chunk, 0:256], w_d[p, 0])
            for n in range(1, 4):
                total = total + dotf(hidden[chunk, 256 * n : 256 * n + 256], w_d[p, n])
            parts = parts + lane_tiles(total)
        for n, value in enumerate(natural_order(parts)):
            psend[0, b, :, 128 * n : 128 * n + 128] = value.astype(BF16)

    repeat(4, down)
    mix_copies = pair_partial(None, psend.at[0], precv.at[0], 12)

    def weight_grad(left, left_rows, grads):
        def turn(j):
            left_t[tile(j, 128, 128), :] = left(tile(j, 128, 128)).T

        repeat(left_rows // 128, turn)
        for grad, dest, count in grads:
            def part(n):
                dest(n, dotf(left_t[0:left_rows], grad(n)))

            repeat(count, part)

    def into(lead_of, first):
        def put(n, value):
            gw[lead_of(n), :, tile(first(n), 128, 128)] = value.astype(BF16)
        return put

    def pack_first(value, a, b):
        return jnp.where(low, value, a.astype(F32)).astype(BF16), jnp.where(low, b.astype(F32), value).astype(BF16)

    def pack_second(value, a, b):
        value = roll_half(value)
        return jnp.where(low, a.astype(F32), value).astype(BF16), jnp.where(low, value, b.astype(F32)).astype(BF16)

    def into_pair(group, pack):
        def put(n, value):
            cols = tile(n + 3 * group, 128, 128)
            gw[0, :, cols], gw[1, :, cols] = pack(value, gw[0, :, cols], gw[1, :, cols])
        return put

    def cols_of(ref, first=0):
        return lambda n: ref[:, tile(n + first, 128, 128)]

    weight_grad(lambda j: nc[:, j], D, [
        (cols_of(gg), into(lambda n: lax.div(n, 4), lambda n: 12 + lax.rem(n, 4)), 8),
        (cols_of(gu), into(lambda n: lax.div(n, 4), lambda n: 16 + lax.rem(n, 4)), 8),
    ])

    def put_down(xs, own_half):
        def put(n, value):
            cols = tile(n, 128, 128)
            top, bottom = value[0:256], roll_half(value[256:512])
            a, b = jnp.where(low, top, bottom).astype(BF16), jnp.where(low, bottom, top).astype(BF16)
            if own_half:
                rows = tile(c + 2 * xs, 256, 256)
                gwd[0, rows, cols] = a
                gwd[1, rows, cols] = b
            else:
                gdsend[xs, 0, :, cols] = a
                gdsend[xs, 1, :, cols] = b
        return put

    gd_copies = []
    for xs in range(2):
        weight_grad(lambda j: hidden[:, pl.ds(pl.multiple_of(j.start + 512 * xs, 128), 128)], 512, [
            (lambda n: ffb[:, tile(n + 3 * (1 - c), 128, 128)], put_down(xs, False), 3),
            (lambda n: ffb[:, tile(n + 3 * c, 128, 128)], put_down(xs, True), 3),
        ])
        gd_copies.append(remote(gdsend.at[xs], gwd.at[:, tile(c + 2 * xs, 256, 256)], 38 + xs, mate))

    wait_all(gc_copies)
    small[...] = jnp.zeros_like(small)

    def keep_gain(index, i, gain):
        small[index : index + 1, 0:D] += jnp.where(lax.rem(i, 2) == c, gain, 0.0)

    def keep_sliced(chunk, total):
        for n, value in enumerate(sliced_order(lane_tiles(total))):
            gxb[chunk, 128 * n : 128 * n + 128] = value.astype(BF16)

    def back_heads(weight):
        for t in range(3):
            first, second = tile(3 * c + t, 64, 64), tile(3 * c + t + 6, 64, 64)
            part = None
            for p in range(2):
                rows = jnp.concatenate([weight[p, first], weight[p, second]], axis=0)
                term = dot_t(gxb[:, H * p : H * p + H], rows)
                part = term if part is None else part + term
            gatt[:, 128 * t : 128 * t + 128] = part.astype(BF16)

    def third(i):
        chunk = tile(i, 128, 128)
        upstream = gsend[chunk].astype(F32) + grecv[chunk].astype(F32)
        gv, gain = norm_back(x2[chunk], gains[2:3], upstream)
        total = full[2, chunk].astype(F32) + gv
        gx2[chunk] = total
        keep_sliced(chunk, total)
        keep_gain(2, i, gain)

    repeat(4, third)
    back_heads(w_co)
    gmkv = grecv
    copies = []
    for t in range(3):
        attend_back(t, cq, 0, mkv, 0, mkv, 3, p_cross, catt, False, gcq, 3 * c, gmkv, 0, gmkv, 3)
        copies.append(send_head(gcq, t, 14))

    mem_copies = pair_partial(lambda k: dot_t(gmkv[:, 0:H], w[0, k, 2 * H : 3 * H]) + dot_t(gmkv[:, H:], w[1, k, 2 * H : 3 * H]), psend.at[1], precv.at[1], 17)

    wait_all(mix_copies)

    def mixed_block(k, chunk):
        return (x2[chunk] + psend[0, 2 * k + c].astype(F32) + precv[0, k].astype(F32)).astype(BF16)

    msend[0] = mixed_block(1 - x, other)
    mix_out = remote(msend.at[0], mixed.at[x], 19, across)
    mixed[x] = mixed_block(x, own)

    weight_grad(lambda j: cattn[:, j], D, [(cols_of(gxb, 3 * c), into_pair(3, pack_second), 3)])
    wait_all(copies)

    def back_b(n):
        cols = tile(n, 256, 256)
        x2[:, cols] = dot_t(gcq[:, 0:H], w_cq[0, cols]) + dot_t(gcq[:, H:], w_cq[1, cols])

    repeat(3, back_b)

    def second(i):
        chunk = tile(i, 128, 128)
        gv, gain = norm_back(x1[chunk], gains[1:2], x2[chunk])
        total = gx2[chunk] + gv
        gx2[chunk] = total
        keep_sliced(chunk, total)
        keep_gain(1, i, gain)

    repeat(4, second)
    back_heads(w_o)
    for t in range(3):
        attend_back(t, qkv, 0, qkv, 3, qkv, 6, p_self, att, True, gg, 0, gg, 3, gu, 0)

    def back_a(k):
        part = dot_t(gg[:, 0:H], w[0, k, 0:H]) + dot_t(gg[:, H : 2 * H], w[1, k, 0:H])
        return part + dot_t(gu[:, 0:H], w[0, k, H : 2 * H])

    ig_copies = pair_partial(back_a, psend.at[2], precv.at[2], 21)

    weight_grad(lambda j: full[1, :, j], D, [
        (cols_of(gmkv), into_pair(2, pack_first), 3), (cols_of(gmkv, 3), into_pair(2, pack_second), 3)])
    norm(lambda k: x1[k], 1, nb)
    weight_grad(lambda j: nb[:, j], D, [(cols_of(gcq, 3 * c), into_pair(1, pack_second), 3)])
    weight_grad(lambda j: attn[:, j], D, [(cols_of(gxb, 3 * c), into_pair(3, pack_first), 3)])
    norm(lambda k: full[0, k].astype(F32), 0, na)
    weight_grad(lambda j: na[:, j], D, [
        (cols_of(gg), into_pair(0, pack_first), 3), (cols_of(gg, 3), into_pair(0, pack_second), 3),
        (cols_of(gu), into_pair(1, pack_first), 3)])

    flipped = (
        lax.broadcasted_iota(jnp.int32, (T, T), 0) + lax.broadcasted_iota(jnp.int32, (T, T), 1) == T - 1
    ).astype(F32)
    by_bucket = (
        jnp.broadcast_to(buckets[...], (128, T)) == lax.broadcasted_iota(jnp.int32, (128, T), 0)
    ).astype(F32)
    high = lax.Precision.HIGHEST
    distances = jnp.dot(dist_grad[...], flipped, precision=high, preferred_element_type=F32)
    per_head = lax.dot_general(
        distances, by_bucket, (((1,), (1,)), ((), ())), precision=high, preferred_element_type=F32)
    for t in range(3):
        for a in range(2):
            here = lax.broadcasted_iota(jnp.int32, (16, 128), 0) == 3 * (2 * a + c) + t
            small[:, D:] += jnp.where(here, per_head[2 * t + a : 2 * t + a + 1], 0.0)

    wait_all(mem_copies)
    msend[1] = (psend[1, 2 * (1 - x) + c].astype(F32) + precv[1, 1 - x].astype(F32)).astype(BF16)
    mem_out = remote(msend.at[1], late.at[0], 20, across)
    memory_grad[x] = psend[1, 2 * x + c].astype(F32) + precv[1, x].astype(F32)

    wait_all(ig_copies)

    def first_block(k, chunk):
        upstream = psend[2, 2 * k + c].astype(F32) + precv[2, k].astype(F32)
        gv, gain = norm_back(full[0, chunk].astype(F32), gains[0:1], upstream)
        small[0:1, 0:D] += gain
        return gx2[chunk] + gv

    msend[2] = first_block(1 - x, other).astype(BF16)
    ig_out = remote(msend.at[2], late.at[1], 23, across)
    input_grad[x] = first_block(x, own)

    mem_out.wait_recv()
    memory_grad[1 - x] = late[0].astype(F32)
    ig_out.wait_recv()
    input_grad[1 - x] = late[1].astype(F32)
    mix_out.wait_recv()
    wait_all(gd_copies)
    for copy in started + weights.sent:
        copy.wait_send()


def layer(blocks, segments, buckets, pos_bias, w, wd, inside):
    def bf(*shape):
        return VMEM(shape, BF16)

    def fl(*shape):
        return VMEM(shape, F32)

    outs = [
        ((2, 128, D), BF16), ((2, 128, D), F32), ((2, 128, D), F32), ((16, D + 128), F32),
        ((2, D, 2688), BF16), ((2, FH, H), BF16),
    ]
    whole = pl.BlockSpec(memory_space=pltpu.VMEM)
    dma = pltpu.SemaphoreType.DMA
    gather_sems = [dma((len(GATHER), 15)), dma((len(GATHER), 15))] if inside else [dma((2,)), dma((2,))]
    return pl.pallas_call(
        functools.partial(layer_kernel, inside),
        out_shape=[jax.ShapeDtypeStruct(s, d) for s, d in outs],
        in_specs=[whole] * 6 + [whole if inside else pl.BlockSpec(memory_space=pl.ANY)] * 2,
        out_specs=[whole] * len(outs),
        scratch_shapes=[
            bf(2, D, H), bf(2, D, H), bf(2, D, H), bf(2, 4, 256, H), fl(8, D), fl(8, T), fl(8, T),
            bf(3, T, D), bf(T, D), bf(T, D), bf(T, 3 * H), bf(T, D), bf(T, D), fl(T, D),
            bf(T, H), bf(T, D), bf(T, D), bf(T, D), fl(T, D),
            bf(6, T, T), bf(6, T, T), bf(T, FH), bf(T, FH), bf(T, FH), bf(T, D), bf(T, D),
            fl(T, D), bf(T, D),
            bf(T, D), fl(128, T), fl(128, T), bf(128, T), bf(128, T),
            bf(D, T), fl(T, T),
            bf(3, 4, 128, D), bf(3, 2, 128, D), bf(3, 128, D), bf(2, 128, D), bf(2, 2, 256, H),
            pltpu.SemaphoreType.DMA((40,)), pltpu.SemaphoreType.DMA((40,)), *gather_sems,
        ],
        input_output_aliases={},
        compiler_params=pltpu.CompilerParams(
            collective_id=0, has_side_effects=True, vmem_limit_bytes=67043328),
        name="layer",
    )(*blocks, segments, buckets.reshape(1, T), pos_bias, w, wd)


PAIRS = ((0, 1), (2, 4), (5, 6), (3, 7))


def pack_pair(a, b, x):
    n = a.shape[0]
    both = jnp.stack([a.reshape(n, 3, 64), b.reshape(n, 3, 64)], axis=2)
    return jnp.where(x == 0, both, both[:, :, ::-1]).reshape(n, H)


def unpack_pair(v, x):
    both = v.reshape(v.shape[0], 3, 2, 64)
    both = jnp.where(x == 0, both, both[:, :, ::-1])
    return both[:, :, 0].reshape(-1, 192), both[:, :, 1].reshape(-1, 192)


def hidden_order(v, half, forward=True):
    n = v.shape[0]
    outer = v.shape[1] // (2 * half)
    v = v.reshape((n, outer, 2, half) if forward else (n, 2, outer, half))
    return v.transpose(0, 2, 1, 3).reshape(n, -1)


def payload(squares, gate, up, down, gains, x):
    half = down.shape[0] // 2
    parts = [pack_pair(squares[a], squares[b], x) for a, b in PAIRS]
    parts += [hidden_order(gate, half), hidden_order(up, half)]
    parts.append(jnp.pad(gains.T, ((0, 0), (0, 125))))
    return jnp.concatenate(parts, axis=1), pack_pair(down[:half], down[half:], x)


def gather_plain(v):
    v = lax.all_gather(v, "rows", axis=0, tiled=True)
    return lax.all_gather(v, "seq", axis=0, axis_index_groups=[[0, 2], [1, 3]])


def reduce_kernel(
    gw, gwd, small_in, *refs,
):
    squares, (gate, up, down, total), refs = refs[:8], refs[8:12], refs[12:]
    r1, r1d, r2, r2d, r3, r3d, acc, got, ssem, rsem, small_ssem, small_rsem = refs
    z, y, x, c = place()
    mate = device(z, y, x, 1 - c)
    y_peer, x_peer = device(z, 1 - y, x, c), device(z, y, 1 - x, c)
    z_peers = [device(lax.rem(z + j, 4), y, x, c) for j in range(1, 4)]
    low = low_lanes()

    barrier = pltpu.get_barrier_semaphore()
    for peer in [mate, y_peer, x_peer] + z_peers:
        pl.semaphore_signal(barrier, inc=1, device_id=peer, device_id_type=MESH)
    pl.semaphore_wait(barrier, 6)
    sent = []

    def copy(k, slot, src, dst, peer):
        return pltpu.make_async_remote_copy(
            src_ref=src, dst_ref=dst, send_sem=ssem.at[k, slot], recv_sem=rsem.at[k, slot],
            device_id=peer, device_id_type=MESH)

    def send(*args):
        out = copy(*args)
        out.start()
        sent.append(out)
        return out

    def part(k, w_ref, d_ref, *lead):
        kind, first, size, _ = SCATTER[k]
        if kind == "w":
            return w_ref.at[(*lead, slice(None), slice(first, first + size))]
        return d_ref.at[(*lead, slice(first, first + size), slice(None))]

    def grads(k, a, mine):
        if SCATTER[k][3]:
            return part(k, gw, gwd, a, slice(None), y if mine else 1 - y)
        return part(k, gw, gwd, x if mine else 1 - x, slice(None), a)

    def second_place(k):
        return x if SCATTER[k][3] else y

    def sides(k):
        m = second_place(k)
        return (1 - m, m)

    def first_send(k):
        peer = y_peer if SCATTER[k][3] else x_peer
        for i, a in enumerate(sides(k)):
            send(k, i, grads(k, a, False), part(k, r1, r1d, a, slice(None)), peer)

    def add_blocks(dest, other):
        def one(i):
            dest[i] = (dest[i].astype(F32) + other[i].astype(F32)).astype(BF16)

        repeat(4, one)

    def after_first(k):
        peer = y_peer if SCATTER[k][3] else x_peer
        onward = x_peer if SCATTER[k][3] else y_peer
        for i, a in enumerate(sides(k)):
            block = part(k, r1, r1d, a, slice(None))
            copy(k, i, block, block, peer).wait_recv()
            add_blocks(block, grads(k, a, True))
            if i == 0:
                send(k, 2, block, part(k, r2, r2d, slice(None)), onward)

    def after_second(k):
        onward = x_peer if SCATTER[k][3] else y_peer
        block = part(k, r2, r2d, slice(None))
        copy(k, 2, block, block, onward).wait_recv()
        add_blocks(block, part(k, r1, r1d, second_place(k), slice(None)))
        for j in range(1, 4):
            send(k, 2 + j, part(k, r2, r2d, lax.rem(z + j, 4)), part(k, r3, r3d, j - 1), z_peers[j - 1])

    def after_third(k):
        value = part(k, r2, r2d, z)[...].astype(F32)
        for j in range(1, 4):
            block = part(k, r3, r3d, j - 1)
            copy(k, 2 + j, block, block, z_peers[j - 1]).wait_recv()
            value = value + block[...].astype(F32)
        kind, first, size, _ = SCATTER[k]
        if kind == "w" and first >= 1536:
            dest = gate if first == 1536 else up
            for n, m in enumerate((0, 2, 1, 3)):
                dest[:, 128 * m : 128 * m + 128] = value[:, 128 * n : 128 * n + 128]
            return
        tiles = [jnp.where(x == 0, v, roll_half(v)) for v in lane_tiles(value)]
        turned = [roll_half(v) for v in tiles]
        if kind == "w":
            one, two = PAIRS[first // H]
            targets = ((squares[one], slice(0, 96)), (squares[two], slice(0, 96)))
        else:
            targets = ((down, slice(first, first + size)), (down, slice(128 + first, 128 + first + size)))
        ref, rows = targets[0]
        ref[rows, 0:128] = jnp.where(low, tiles[0], turned[1])
        ref[rows, 128:192] = tiles[2][:, 0:64]
        ref, rows = targets[1]
        ref[rows, 0:128] = jnp.where(low, turned[0], tiles[1])
        ref[rows, 128:192] = turned[2][:, 0:64]

    def small_send(slot, src, peer):
        out = pltpu.make_async_remote_copy(
            src_ref=src, dst_ref=got.at[slot], send_sem=small_ssem.at[slot], recv_sem=small_rsem.at[slot],
            device_id=peer, device_id_type=MESH)
        out.start()
        sent.append(out)
        return out

    count = len(SCATTER)
    first = small_send(0, small_in, mate)
    for k in range(count):
        first_send(k)
    first.wait_recv()
    acc[0] = small_in[...] + got[0]
    first = small_send(1, acc.at[0], x_peer)
    after_first(0)
    first.wait_recv()
    acc[1] = acc[0] + got[1]
    first = small_send(2, acc.at[1], y_peer)
    after_first(1)
    after_second(0)
    first.wait_recv()
    acc[2] = acc[1] + got[2]
    last = [small_send(2 + j, acc.at[2], z_peers[j - 1]) for j in range(1, 4)]
    for k in range(2, count):
        after_first(k)
        after_second(k - 1)
        after_third(k - 2)
    after_second(count - 1)
    after_third(count - 2)
    after_third(count - 1)
    for out in last:
        out.wait_recv()
    total[...] = acc[2] + got[3] + got[4] + got[5]
    for out in sent:
        out.wait_send()


def scatter_lines(gw, gwd, small, x):
    def bf(*shape):
        return VMEM(shape, BF16)

    whole = pl.BlockSpec(memory_space=pltpu.VMEM)
    dma = pltpu.SemaphoreType.DMA
    outs = [(96, 192)] * 8 + [(96, 512), (96, 512), (256, 192), small.shape]
    out = pl.pallas_call(
        reduce_kernel,
        out_shape=[jax.ShapeDtypeStruct(s, F32) for s in outs],
        in_specs=[whole] * 3,
        out_specs=[whole] * len(outs),
        scratch_shapes=[
            bf(2, 4, 96, 2560), bf(2, 4, 128, H), bf(4, 96, 2560), bf(4, 128, H), bf(3, 96, 2560), bf(3, 128, H),
            VMEM((3,) + small.shape, F32), VMEM((6,) + small.shape, F32),
            dma((len(SCATTER), 6)), dma((len(SCATTER), 6)), dma((6,)), dma((6,)),
        ],
        compiler_params=pltpu.CompilerParams(
            collective_id=1, has_side_effects=True, vmem_limit_bytes=60000000),
        name="reduce",
    )(gw.reshape(2, 4, 2, 96, 2688), gwd.reshape(2, 4, 2, 128, H), small)
    return list(out[:8]), *out[8:]


def scatter_plain(gw, gwd, small, x):
    gw = gw[:, :, :2560]

    def reduced(v):
        v = lax.psum_scatter(v, "rows", scatter_dimension=1, tiled=True)
        kept = lax.dynamic_index_in_dim(v, x, 0, keepdims=False).astype(F32)
        sent = lax.dynamic_index_in_dim(v, 1 - x, 0, keepdims=False)
        return kept + lax.ppermute(sent, "seq", [(0, 2), (2, 0), (1, 3), (3, 1)]).astype(F32)

    total, down = reduced(gw), reduced(gwd)
    half = down.shape[0]
    squares = [None] * 8
    for k, (a, b) in enumerate(PAIRS):
        squares[a], squares[b] = unpack_pair(total[:, H * k : H * k + H], x)
    gate = hidden_order(total[:, 1536:2048], half, False)
    up = hidden_order(total[:, 2048:], half, False)
    down = jnp.concatenate(unpack_pair(down, x), axis=0)
    return squares, gate, up, down, lax.psum(small, ("rows", "seq"))


def shards(
    layer_input, memory, output_grad, segments, buckets,
    self_query, self_key, self_value, self_output,
    cross_query, cross_key, cross_value, cross_output,
    gate_weight, up_weight, down_weight, norm_gains, position_bias,
):
    x = lax.axis_index("seq") // 2
    squares = (self_query, self_key, self_value, self_output, cross_query, cross_key, cross_value, cross_output)
    w, wd = payload(squares, gate_weight, up_weight, down_weight, norm_gains, x)
    inside = lax.axis_size("rows") == 8
    if not inside:
        w, wd = gather_plain(w), gather_plain(wd)
    mixed, input_grad, memory_grad, small, gw, gwd = layer(
        (layer_input, memory, output_grad), segments, buckets, position_bias, w, wd, inside)
    scatter = scatter_lines if inside else scatter_plain
    squares, gate, up, down, small = scatter(gw, gwd, small, x)
    width = D // lax.axis_size("rows")
    gains = lax.dynamic_slice(small, (0, lax.axis_index("rows") * width), (3, width))
    return (mixed, input_grad, memory_grad, *squares, gate, up, down, gains, small[:HEADS, D : D + BUCKETS].T)


def solution(mesh):
    tokens = P("rows", "seq", None)
    weight = P("rows", "seq")
    return jax.shard_map(
        shards,
        mesh=mesh,
        in_specs=(tokens, tokens, tokens, P("rows", None), P()) + (weight,) * 11 + (P(None, "rows"), P()),
        out_specs=(tokens,) * 3 + (weight,) * 11 + (P(None, "rows"), P()),
        check_vma=False,
    )
```

```python
import functools

import jax
import jax.numpy as jnp
from jax import lax
from jax.experimental import pallas as pl
from jax.experimental.pallas import tpu as pltpu
from jax.sharding import PartitionSpec as P

HEADS = 12
BUCKETS = 32
EPS = 1e-06
NEG = -1e30
F32 = jnp.float32
BF16 = jnp.bfloat16
MESH = pl.DeviceIdType.MESH
T = 512
D = 768
H = 384
FH = 1024
VMEM = pltpu.VMEM


def dotf(a, b):
    return jnp.dot(a, b, preferred_element_type=F32)


def dot_t(a, b):
    return lax.dot_general(a, b, (((1,), (1,)), ((), ())), preferred_element_type=F32)


def repeat(count, body):
    lax.fori_loop(0, count, lambda i, carry: (body(i), carry)[1], 0)


def tile(start, step, size):
    return pl.ds(pl.multiple_of(start * step, step), size)


def rms_scale(v):
    return lax.rsqrt(jnp.mean(v * v, axis=-1, keepdims=True) + EPS)


def norm_back(v, gain, upstream):
    r = rms_scale(v)
    scaled = gain * upstream
    gv = r * scaled - v * (r * r * r) * jnp.mean(scaled * v, axis=-1, keepdims=True)
    return gv, jnp.sum(upstream * v * r, axis=0, keepdims=True)


def roll_half(v):
    return pltpu.roll(v, 64, 1)


def low_lanes():
    return lax.broadcasted_iota(jnp.int32, (1, 128), 1) < 64


def sliced_order(tiles):
    low = low_lanes()
    out = []
    for n in range(6):
        a, b = tiles[n // 2], tiles[n // 2 + 3]
        out.append(jnp.where(low, a, roll_half(b)) if n % 2 == 0 else jnp.where(low, roll_half(a), b))
    return out


def natural_order(tiles):
    low = low_lanes()
    out = [jnp.where(low, tiles[2 * k], roll_half(tiles[2 * k + 1])) for k in range(3)]
    return out + [jnp.where(low, roll_half(tiles[2 * k]), tiles[2 * k + 1]) for k in range(3)]


def lane_tiles(v):
    return [v[:, 128 * n : 128 * n + 128] for n in range(v.shape[1] // 128)]


GATHER = (
    ("w", 2560, 128, 0), ("w", 0, H, 0), ("w", H, H, 1), ("w", 2 * H, H, 0), ("w", 3 * H, H, 1),
    ("d", 0, 64, 0), ("d", 64, 64, 1), ("w", 1536, 512, 0), ("w", 2048, 512, 1),
)
SCATTER = (
    ("w", 1536, 512, 0), ("w", 2048, 512, 1), ("d", 0, 64, 0), ("d", 64, 64, 1),
    ("w", 2 * H, H, 0), ("w", 3 * H, H, 1), ("w", 0, H, 0), ("w", H, H, 1),
)


OWN = {
    ("w", 0): (0, 0), ("w", H): (0, H), ("w", 2560): (0, 2 * H), ("w", 2 * H): (96, 0), ("w", 3 * H): (96, H),
    ("w", 1536): (192, 0), ("w", 2048): (192, 512), ("d", 0): (288, 0), ("d", 64): (352, 0),
}


def place():
    row, seq = lax.axis_index("rows"), lax.axis_index("seq")
    return lax.div(row, 2), lax.rem(row, 2), lax.div(seq, 2), lax.rem(seq, 2)


def device(z, y, x, c):
    return (2 * z + y, 2 * x + c)


class Gather:
    def __init__(self, room, w, wd, ssem, rsem):
        self.refs = (room, w, wd, ssem, rsem)
        self.z, self.y, self.x, self.c = place()
        self.sent = []
        self.open = {}
        self.todo = []
        count = len(GATHER)
        for k in range(min(3, count)):
            self.todo.append((self.begin, k))
        for k in range(count):
            self.todo.append((self.after_z, k))
            if k + 3 < count:
                self.todo.append((self.begin, k + 3))
            if k >= 1:
                self.todo.append((self.after_p, k - 1))
            if k >= 2:
                self.todo.append((self.finish, k - 2))
        self.todo += [(self.after_p, count - 1), (self.finish, count - 2), (self.finish, count - 1)]
        self.done = -1

    def view(self, k, x, z, y):
        kind, first, size, _ = GATHER[k]
        _, w, wd, _, _ = self.refs
        r = 2 * z + y
        if kind == "w":
            return w.at[x, pl.ds(pl.multiple_of(96 * r, 96), 96), first : first + size]
        return wd.at[x, pl.ds(pl.multiple_of(128 * r + first, 64), size), :]

    def own(self, k):
        kind, first, size, _ = GATHER[k]
        row, lane = OWN[kind, first]
        height, width = (96, size) if kind == "w" else (size, H)
        return self.refs[0].at[row : row + height, lane : lane + width]

    def peers(self, k):
        y_peer, x_peer = device(self.z, 1 - self.y, self.x, self.c), device(self.z, self.y, 1 - self.x, self.c)
        return (x_peer, y_peer) if GATHER[k][3] else (y_peer, x_peer)

    def across_p(self, k):
        return (1 - self.x, self.y) if GATHER[k][3] else (self.x, 1 - self.y)

    def copy(self, k, slot, src, dst, peer):
        _, _, _, ssem, rsem = self.refs
        return pltpu.make_async_remote_copy(
            src_ref=src, dst_ref=dst, send_sem=ssem.at[k, slot], recv_sem=rsem.at[k, slot],
            device_id=peer, device_id_type=MESH)

    def send(self, k, *args):
        copy = self.copy(k, *args)
        copy.start()
        self.open[k].append(copy)

    def behind(self, j):
        return lax.rem(self.z + 4 - j, 4)

    def begin(self, k):
        here = self.view(k, self.x, self.z, self.y)
        p, q = self.peers(k)
        own = self.own(k)
        self.open[k] = []
        self.send(k, 3, own, here, p)
        self.send(k, 7, own, here, q)
        for j in range(1, 4):
            self.send(k, j - 1, own, here, device(lax.rem(self.z + j, 4), self.y, self.x, self.c))
        here[...] = own[...]

    def after_z(self, k):
        p, q = self.peers(k)
        for j in range(1, 4):
            block = self.view(k, self.x, self.behind(j), self.y)
            self.copy(k, j - 1, block, block, p).wait_recv()
            self.send(k, 3 + j, block, block, p)
            self.send(k, 7 + j, block, block, q)

    def after_p(self, k):
        p, q = self.peers(k)
        x, y = self.across_p(k)
        for j in range(4):
            block = self.view(k, x, self.behind(j), y)
            self.copy(k, 3 + j, block, block, p).wait_recv()
            self.send(k, 11 + j, block, block, q)

    def finish(self, k):
        p, q = self.peers(k)
        x, y = (self.x, 1 - self.y) if GATHER[k][3] else (1 - self.x, self.y)
        for j in range(4):
            block = self.view(k, x, self.behind(j), y)
            self.copy(k, 7 + j, block, block, q).wait_recv()
        for j in range(4):
            block = self.view(k, 1 - self.x, self.behind(j), 1 - self.y)
            self.copy(k, 11 + j, block, block, q).wait_recv()
        for copy in self.open[k]:
            copy.wait_send()
        self.done = k

    def pump(self, count):
        for _ in range(min(count, len(self.todo))):
            action, k = self.todo.pop(0)
            action(k)

    def need(self, k):
        while self.done < k:
            self.pump(1)


class Scatter:
    def __init__(self, w, wd, sums, buffers, ssem, rsem):
        self.grads, self.sums = (w, wd), sums
        self.buffers = (buffers[0:2], buffers[2:4], buffers[4:6])
        self.sems = (ssem, rsem)
        self.z, self.y, self.x, self.c = place()
        self.y_peer = device(self.z, 1 - self.y, self.x, self.c)
        self.x_peer = device(self.z, self.y, 1 - self.x, self.c)
        self.z_peers = [device(lax.rem(self.z + j, 4), self.y, self.x, self.c) for j in range(1, 4)]
        self.sent = []
        self.ready = set()
        count = len(SCATTER)
        self.todo = [(self.first, n) for n in range(4)]
        for n in range(count):
            self.todo.append((self.after_first, n))
            if n + 4 < count:
                self.todo.append((self.first, n + 4))
            if n >= 1:
                self.todo.append((self.after_second, n - 1))
            if n >= 2:
                self.todo.append((self.after_third, n - 2))
        self.todo += [(self.after_second, count - 1), (self.after_third, count - 2), (self.after_third, count - 1)]

    def copy(self, n, slot, src, dst, peer):
        ssem, rsem = self.sems
        return pltpu.make_async_remote_copy(
            src_ref=src, dst_ref=dst, send_sem=ssem.at[n, slot], recv_sem=rsem.at[n, slot],
            device_id=peer, device_id_type=MESH)

    def send(self, *args):
        copy = self.copy(*args)
        copy.start()
        self.sent.append(copy)

    def part(self, n, refs, *lead):
        kind, first, size, _ = SCATTER[n]
        if kind == "w":
            return refs[0].at[(*lead, slice(None), slice(first, first + size))]
        return refs[1].at[(*lead, slice(first, first + size), slice(None))]

    def grad(self, n, a, z, mine):
        kind, first, size, order = SCATTER[n]
        x, y = (a, self.y if mine else 1 - self.y) if order else (self.x if mine else 1 - self.x, a)
        r = 2 * z + y
        if kind == "w":
            return self.grads[0].at[x, pl.ds(pl.multiple_of(96 * r, 96), 96), first : first + size]
        return self.grads[1].at[x, pl.ds(pl.multiple_of(128 * r + first, 64), size), :]

    def second_place(self, n):
        return self.x if SCATTER[n][3] else self.y

    def first(self, n):
        peer = self.y_peer if SCATTER[n][3] else self.x_peer
        m = self.second_place(n)
        for i, a in enumerate((1 - m, m)):
            for z in range(4):
                self.send(n, 4 * i + z, self.grad(n, a, z, False), self.part(n, self.buffers[0], a, z), peer)

    def add(self, dest, other):
        dest[...] = (dest[...].astype(F32) + other[...].astype(F32)).astype(BF16)

    def after_first(self, n):
        peer, onward = (self.y_peer, self.x_peer) if SCATTER[n][3] else (self.x_peer, self.y_peer)
        m = self.second_place(n)
        for i, a in enumerate((1 - m, m)):
            for z in range(4):
                block = self.part(n, self.buffers[0], a, z)
                self.copy(n, 4 * i + z, block, block, peer).wait_recv()

            def one(z):
                self.add(self.part(n, self.buffers[0], a, z), self.grad(n, a, z, True))

            repeat(4, one)
            if i == 0:
                block = self.part(n, self.buffers[0], a, slice(None))
                self.send(n, 8, block, self.part(n, self.buffers[1], slice(None)), onward)

    def after_second(self, n):
        onward = self.x_peer if SCATTER[n][3] else self.y_peer
        block = self.part(n, self.buffers[1], slice(None))
        self.copy(n, 8, block, block, onward).wait_recv()
        m = self.second_place(n)

        def one(z):
            self.add(self.part(n, self.buffers[1], z), self.part(n, self.buffers[0], m, z))

        repeat(4, one)
        for j in range(1, 4):
            self.send(
                n, 8 + j, self.part(n, self.buffers[1], lax.rem(self.z + j, 4)),
                self.part(n, self.buffers[2], j - 1), self.z_peers[j - 1])

    def after_third(self, n):
        value = self.part(n, self.buffers[1], self.z)[...].astype(F32)
        for j in range(1, 4):
            block = self.part(n, self.buffers[2], j - 1)
            self.copy(n, 8 + j, block, block, self.z_peers[j - 1]).wait_recv()
            value = value + block[...].astype(F32)
        self.part(n, self.sums)[...] = value

    def made(self, *pieces):
        self.ready.update(pieces)
        self.pump(0)

    def pump(self, count):
        while self.todo:
            action, n = self.todo[0]
            if action == self.first:
                if n not in self.ready:
                    return
            elif count <= 0:
                return
            else:
                count -= 1
            self.todo.pop(0)
            action(n)


class Idle:
    def __init__(self):
        self.sent = []

    def made(self, *pieces):
        pass

    def pump(self, count):
        pass


class Loaded:
    def __init__(self, w_in, wd_in, w, wd, sems):
        self.copies = [pltpu.make_async_copy(w_in, w, sems.at[0]), pltpu.make_async_copy(wd_in, wd, sems.at[1])]
        for copy in self.copies:
            copy.start()
        self.sent = []

    def pump(self, count):
        pass

    def need(self, k):
        for copy in self.copies:
            copy.wait()
        self.copies = []


def pair_tiles(a, b, x):
    low = low_lanes()
    tiles = []
    for t in range(3):
        u, v = [m[:, 64 * t : 64 * t + 64].astype(F32) for m in (a, b)]
        tiles.append(jnp.where(x == 0, jnp.concatenate([u, v], axis=1), jnp.concatenate([v, u], axis=1)))
    return tiles


def fill_payload(packed, room, x):
    squares, gate, up, down, gains = packed[:8], packed[8], packed[9], packed[10], packed[11]
    for n, (a, b) in enumerate(PAIRS):
        for t, value in enumerate(pair_tiles(squares[a][...], squares[b][...], x)):
            rows, lanes = OWN["w", H * n]
            room[rows : rows + 96, lanes + 128 * t : lanes + 128 * t + 128] = value.astype(BF16)
    for ref, first in ((gate, 1536), (up, 2048)):
        rows, lanes = OWN["w", first]
        for n, m in enumerate((0, 2, 1, 3)):
            room[rows : rows + 96, lanes + 128 * n : lanes + 128 * n + 128] = ref[:, 128 * m : 128 * m + 128]
    rows, lanes = OWN["d", 0]
    for t, value in enumerate(pair_tiles(down[0:128], down[128:256], x)):
        room[rows : rows + 128, lanes + 128 * t : lanes + 128 * t + 128] = value.astype(BF16)
    spread = lax.broadcasted_iota(jnp.int32, (3, 128), 0) == lax.broadcasted_iota(jnp.int32, (3, 128), 1)
    columns = lax.dot_general(
        gains[...], spread.astype(BF16), (((0,), (0,)), ((), ())), preferred_element_type=F32)
    rows, lanes = OWN["w", 2560]
    room[rows : rows + 96, lanes : lanes + 128] = columns.astype(BF16)


def layer_kernel(
    inside, in_x, in_m, in_g, segments, buckets, pos_bias, *refs,
):
    count = 12 if inside else 2
    packed, refs = refs[:count], refs[count:]
    mixed, input_grad, memory_grad, *refs = refs
    if inside:
        sums, sums_d, total, *refs = refs
    else:
        small, w, wd, *refs = refs
    (
    w_o, w_cq, w_co, w_d, gains, table, dist_grad, full, ffb, na, qkv, att, attn, x1, cq, mkv, catt, x2,
    bias, p_self, hidden, gg, gu, gsend, grecv, gx2, gxb,
    gcq, dk_t, dv_t, qt_s, gt_s, left_t, work,
    psend, precv, msend, late, gdsend,
    ssem, rsem, gather_ssem, gather_rsem,
    ) = refs[:43]
    if inside:
        small, w, wd, acc, got, *refs = refs[43:]
        buffers, (scatter_ssem, scatter_rsem, small_ssem, small_rsem) = refs[:6], refs[6:]
    p_cross = bias
    gw, gwd = w, wd
    nb = nc = na
    cattn = attn
    gatt = hidden
    row = lax.axis_index("rows")
    seq = lax.axis_index("seq")
    x = lax.div(seq, 2)
    c = lax.rem(seq, 2)
    mate = (row, 2 * x + (1 - c))
    across = (row, lax.rem(seq + 2, 4))

    if inside:
        fill_payload(packed, gg, x)

    barrier = pltpu.get_barrier_semaphore()
    peers = [mate, across]
    if inside:
        pz, py, px, pc = place()
        peers.append(device(pz, 1 - py, px, pc))
        peers += [device(lax.rem(pz + j, 4), py, px, pc) for j in range(1, 4)]
    for peer in peers:
        pl.semaphore_signal(barrier, inc=1, device_id=peer, device_id_type=MESH)
    pl.semaphore_wait(barrier, len(peers))

    if inside:
        weights = Gather(gg, w, wd, gather_ssem, gather_rsem)
    else:
        weights = Loaded(packed[0], packed[1], w, wd, gather_ssem)
    weights.pump(3)
    scatter = Idle()
    if inside:
        scatter = Scatter(w, wd, (sums, sums_d), buffers, scatter_ssem, scatter_rsem)
    started = []

    def remote(src, dst, slot, peer, keep=True):
        copy = pltpu.make_async_remote_copy(
            src_ref=src, dst_ref=dst, send_sem=ssem.at[slot], recv_sem=rsem.at[slot],
            device_id=peer, device_id_type=MESH)
        copy.start()
        if keep:
            started.append(copy)
        return copy

    mine = tile(c, H, H)
    low = lax.broadcasted_iota(jnp.int32, (1, 128), 1) < 64
    masks = (low, jnp.logical_not(low))
    flip = (
        lax.broadcasted_iota(jnp.int32, (256, 256), 0)
        + lax.broadcasted_iota(jnp.int32, (256, 256), 1)
        == 255
    ).astype(BF16)

    own = tile(seq, 128, 128)
    other = tile(lax.rem(seq + 2, 4), 128, 128)
    dist_grad[...] = jnp.zeros_like(dist_grad)
    to_across, to_mate = [], []
    for k, block in enumerate((in_x, in_m, in_g)):
        to_across.append(remote(block.at[1 - x], full.at[k, own], 25 + k, across))
        to_mate.append(remote(block.at[x], full.at[k, own], 28 + k, mate))
        full[k, own] = block[x]

    def separate(first, second, ref, lanes, rows_at, count):
        def part(i):
            at = tile(i, 128, 128) if rows_at is None else rows_at(i)
            a, b = ref[0, at, lanes].astype(F32), ref[1, at, lanes].astype(F32)
            first(at, jnp.where(low, a, b).astype(BF16))
            second(at, roll_half(jnp.where(low, b, a)).astype(BF16))

        repeat(count, part)

    def store(ref, lead, lanes):
        def put(at, value):
            ref[lead, at, lanes] = value
        return put

    def separate_group(group):
        for t in range(3):
            lanes = slice(128 * (3 * group + t), 128 * (3 * group + t) + 128)
            inner = slice(128 * t, 128 * t + 128)
            first, second = store(w, 0, lanes), store(w, 1, lanes)
            if group == 1:
                second = store(w_cq, c, inner)
            if group == 3:
                first, second = store(w_o, c, inner), store(w_co, c, inner)
            separate(first, second, w, lanes, None, 6)

    halves = []

    def share(ref, slot):
        halves.append(remote(ref.at[c], ref.at[c], slot, mate))

    def separate_down():
        for t in range(3):
            lanes = slice(128 * t, 128 * t + 128)
            separate(store(wd, 0, lanes), store(wd, 1, lanes), wd, lanes, None, 8)
        copies = []
        for xs in range(2):
            for b in range(2):
                w_d[c, 2 * xs + b] = wd[b, tile(c + 2 * xs, 256, 256)]
                piece = wd.at[b, tile((1 - c) + 2 * xs, 256, 256)]
                copies.append(remote(piece, w_d.at[c, 2 * xs + b], 34 + 2 * xs + b, mate, False))
        return copies

    hot = (lax.broadcasted_iota(jnp.int32, (BUCKETS, T), 0) == buckets[...]).astype(BF16)
    by_distance = lax.dot_general(pos_bias[...], hot, (((0,), (0,)), ((), ())), preferred_element_type=F32)
    both = lax.broadcasted_iota(jnp.int32, (T, T), 0) + lax.broadcasted_iota(jnp.int32, (T, T), 1)
    mirror = ((both == 0) | (both == T)).astype(BF16)
    work[0:HEADS] = dotf(by_distance.astype(BF16), mirror)
    for t in range(3):
        for a in range(2):
            table[2 * t + a : 2 * t + a + 1] = work[pl.ds(3 * (2 * a + c) + t, 1), :]
    seg_row = segments[pl.ds(x, 1), :]
    seg_col = jnp.broadcast_to(seg_row.astype(F32), (128, T)).T[:, 0:1].astype(jnp.int32)

    for qt in range(2):
        rows = slice(256 * qt, 256 * qt + 256)
        qpos = lax.broadcasted_iota(jnp.int32, (256, T), 0) + 256 * qt
        kpos = lax.broadcasted_iota(jnp.int32, (256, T), 1)
        allowed = (kpos <= qpos) & (seg_col[rows, :] == seg_row)
        work[0:256] = jnp.where(allowed, 0.0, NEG)

        def build(h):
            line = jnp.broadcast_to(table[pl.ds(h, 1), :], (256, T))
            line = pltpu.roll(line, 256 * qt, 1, stride=1, stride_axis=0)
            bias[h, rows] = (line + work[0:256]).astype(BF16)

        repeat(6, build)

    relays = []
    for k in range(3):
        to_across[k].wait_recv()
        relays.append(remote(full.at[k, other], full.at[k, other], k, mate))
    for k in range(3):
        to_mate[k].wait_recv()
        relays[k].wait_recv()

    def order_grad(i):
        chunk = tile(i, 128, 128)
        for n, value in enumerate(sliced_order(lane_tiles(full[2, chunk].astype(F32)))):
            ffb[chunk, 128 * n : 128 * n + 128] = value.astype(BF16)

    repeat(4, order_grad)

    def norm(source, gain, dest):
        def part(i):
            chunk = tile(i, 128, 128)
            v = source(chunk)
            dest[chunk] = (v * rms_scale(v) * gains[gain : gain + 1]).astype(BF16)

        repeat(4, part)

    weights.need(0)
    gains[...] = w[0, :, 2560:2688].astype(F32).T[0:8]
    norm(lambda k: full[0, k].astype(F32), 0, na)
    weights.need(1)
    separate_group(0)
    qkv[:, 0:H] = (dotf(na[...], w[0, :, 0:H]).astype(BF16) * 0.125).astype(BF16)
    qkv[:, H : 2 * H] = dotf(na[...], w[1, :, 0:H]).astype(BF16)
    weights.need(2)
    separate_group(1)
    share(w_cq, 31)
    qkv[:, 2 * H :] = dotf(na[...], w[0, :, H : 2 * H]).astype(BF16)

    def prob_place(qt, causal):
        if causal:
            return slice(0, 256), slice(256 * qt, 256 + 512 * qt)
        return slice(256 * qt, 256 * qt + 256), slice(0, T)

    def attend(t, q, qo, k, ko, v, vo, bias_ref, probs, out):
        qc, kc, vc = tile(t + qo, 128, 128), tile(t + ko, 128, 128), tile(t + vo, 128, 128)
        oc = tile(t + 3 * c, 128, 128)
        for qt in range(2):
            rows = slice(256 * qt, 256 * qt + 256)
            nk = T if bias_ref is None else 256 * (qt + 1)
            q2, k2, v2 = q[rows, qc], k[0:nk, kc], v[0:nk, vc]
            outs = []
            for a in range(2):
                s = dot_t(jnp.where(masks[a], q2, jnp.zeros_like(q2)), k2)
                if bias_ref is not None:
                    s = s + bias_ref[2 * t + a, rows, 0:nk].astype(F32)
                e = jnp.exp(s - jnp.max(s, axis=-1, keepdims=True))
                prob = (e * (1.0 / jnp.sum(e, axis=-1, keepdims=True))).astype(BF16)
                at, keys = prob_place(qt, bias_ref is not None)
                probs[2 * t + a, at, keys] = prob
                outs.append(dotf(prob, v2))
            out[rows, oc] = jnp.where(low, outs[0], outs[1]).astype(BF16)

    def attend_back(t, q, qo, k, ko, v, vo, probs, out, causal, gq, gqo, gk, gko, gv, gvo):
        qc, kc, vc = tile(t + qo, 128, 128), tile(t + ko, 128, 128), tile(t + vo, 128, 128)
        oc, gc = tile(t + 3 * c, 128, 128), tile(t, 128, 128)
        qt_s[...] = q[:, qc].T
        gt_s[...] = gatt[:, gc].T
        for qt in (1, 0):
            rows = slice(256 * qt, 256 * qt + 256)
            nk = 256 * (qt + 1) if causal else T
            k2, v2 = k[0:nk, kc], v[0:nk, vc]
            g2 = gatt[rows, gc]
            both = g2.astype(F32) * out[rows, oc].astype(F32)
            outs = []
            for a in range(2):
                half = slice(64 * a, 64 * a + 64)
                delta = jnp.sum(jnp.where(masks[a], both, 0.0), axis=-1, keepdims=True)
                dp = dot_t(jnp.where(masks[a], g2, jnp.zeros_like(g2)), v2)
                at, keys = prob_place(qt, causal)
                prob = probs[2 * t + a, at, keys]
                ds = (prob.astype(F32) * (dp - delta)).astype(BF16)
                outs.append(dotf(ds, k2))
                dk = dotf(qt_s[half, rows], ds)
                dv = dotf(gt_s[half, rows], prob)
                if qt == 1:
                    dk_t[half, :] = dk
                    dv_t[half, :] = dv
                else:
                    dk_t[half, 0:nk] += dk
                    dv_t[half, 0:nk] += dv
                if causal:
                    band = slice(256 * a, 256 * a + 256)
                    if qt == 1:
                        work[band] = dotf(flip, ds)
                    else:
                        work[band, 256:T] += dotf(flip, ds)
                        turned = pltpu.roll(work[band], 0, 1, stride=1, stride_axis=0)
                        dist_grad[pl.ds(2 * t + a, 1), :] = jnp.sum(turned, axis=0, keepdims=True)
            gq[rows, tile(t + gqo, 128, 128)] = (jnp.where(low, outs[0], outs[1]) * 0.125).astype(BF16)
        gk[:, tile(t + gko, 128, 128)] = dk_t[...].T.astype(BF16)
        gv[:, tile(t + gvo, 128, 128)] = dv_t[...].T.astype(BF16)

    def send_head(ref, t, slot):
        cols = tile(t + 3 * c, 128, 128)
        return remote(ref.at[:, cols], ref.at[:, cols], slot + t, mate)

    def wait_all(copies):
        for copy in copies:
            copy.wait_recv()

    copies = []
    for t in range(3):
        attend(t, qkv, 0, qkv, 3, qkv, 6, bias, p_self, att)
        copies.append(send_head(att, t, 3))
        weights.pump(3)

    weights.need(3)
    separate_group(2)
    for k in range(2):
        mkv[:, H * k : H * k + H] = dotf(full[1], w[k, :, 2 * H : 3 * H]).astype(BF16)
    weights.need(4)
    separate_group(3)
    share(w_o, 32)
    share(w_co, 33)
    wait_all(copies)

    def natural_heads(source, dest):
        def part(i):
            chunk = tile(i, 128, 128)
            for n, value in enumerate(natural_order(lane_tiles(source[chunk].astype(F32)))):
                dest[chunk, 128 * n : 128 * n + 128] = value.astype(BF16)

        repeat(4, part)

    def residual(before, heads, weight, dest):
        def part(i):
            chunk = tile(i, 256, 256)
            parts = lane_tiles(dotf(heads[chunk], weight[0])) + lane_tiles(dotf(heads[chunk], weight[1]))
            for n, value in enumerate(natural_order(parts)):
                cols = slice(128 * n, 128 * n + 128)
                dest[chunk, cols] = before(chunk, cols) + value

        repeat(2, part)

    natural_heads(att, attn)
    wait_all(halves)
    residual(lambda r, k: full[0, r, k].astype(F32), attn, w_o, x1)
    norm(lambda k: x1[k], 1, nb)
    cq[...] = (dotf(nb[...], w_cq[c]).astype(BF16) * 0.125).astype(BF16)

    copies = []
    for t in range(3):
        attend(t, cq, 0, mkv, 0, mkv, 3, None, p_cross, catt)
        copies.append(send_head(catt, t, 6))
        weights.pump(2)
    wait_all(copies)

    weights.need(6)
    down_copies = separate_down()
    natural_heads(catt, cattn)
    residual(lambda r, k: x1[r, k], cattn, w_co, x2)
    norm(lambda k: x2[k], 2, nc)

    weights.need(8)
    for copy in down_copies:
        copy.wait()

    def feed(n):
        cols = tile(n, 256, 256)
        xs, b = lax.div(n, 2), lax.rem(n, 2)
        gate = dotf(nc[...], w[xs, :, tile(6 + b, 256, 256)])
        up = dotf(nc[...], w[xs, :, tile(8 + b, 256, 256)])
        back = dot_t(ffb[:, 0:H], w_d[0, n]) + dot_t(ffb[:, H:], w_d[1, n])
        square = gate * gate
        th = jnp.tanh(0.7978845608028654 * gate * (1.0 + 0.044715 * square))
        half = 0.5 * (1.0 + th)
        act = gate * half
        slope = half + 0.5 * gate * (1.0 - th * th) * (0.7978845608028654 * (1.0 + 0.134145 * square))
        hidden[:, cols] = (act * up).astype(BF16)
        gg[:, cols] = (back * up * slope).astype(BF16)
        gu[:, cols] = (back * act).astype(BF16)

    repeat(4, feed)

    gc_copies = []
    for n in range(3):
        cols = slice(256 * n, 256 * n + 256)
        part = dot_t(gg[:, 0:512], w[0, cols, 1536:2048]) + dot_t(gu[:, 0:512], w[0, cols, 2048:2560])
        part = part + dot_t(gg[:, 512:], w[1, cols, 1536:2048]) + dot_t(gu[:, 512:], w[1, cols, 2048:2560])
        gsend[:, cols] = part.astype(BF16)
        gc_copies.append(remote(gsend.at[:, cols], grecv.at[:, cols], 9 + n, mate))

    def pair_partial(product, buf_send, buf_recv, slot):
        def part(n):
            cols = tile(n, 256, 256)
            value = product(cols).astype(BF16)
            for b in range(4):
                buf_send[b, :, cols] = value[128 * b : 128 * b + 128]

        if product is not None:
            repeat(3, part)
        return [remote(buf_send.at[2 * k + (1 - c)], buf_recv.at[k], slot + k, mate) for k in range(2)]

    def down(b):
        chunk = tile(b, 128, 128)
        parts = []
        for p in range(2):
            total = dotf(hidden[chunk, 0:256], w_d[p, 0])
            for n in range(1, 4):
                total = total + dotf(hidden[chunk, 256 * n : 256 * n + 256], w_d[p, n])
            parts = parts + lane_tiles(total)
        for n, value in enumerate(natural_order(parts)):
            psend[0, b, :, 128 * n : 128 * n + 128] = value.astype(BF16)

    repeat(4, down)
    mix_copies = pair_partial(None, psend.at[0], precv.at[0], 12)

    def weight_grad(left, left_rows, grads):
        def turn(j):
            left_t[tile(j, 128, 128), :] = left(tile(j, 128, 128)).T

        repeat(left_rows // 128, turn)
        for grad, dest, count in grads:
            def part(n):
                dest(n, dotf(left_t[0:left_rows], grad(n)))

            repeat(count, part)

    def into(lead_of, first):
        def put(n, value):
            gw[lead_of(n), :, tile(first(n), 128, 128)] = value.astype(BF16)
        return put

    def pack_first(value, a, b):
        return jnp.where(low, value, a.astype(F32)).astype(BF16), jnp.where(low, b.astype(F32), value).astype(BF16)

    def pack_second(value, a, b):
        value = roll_half(value)
        return jnp.where(low, a.astype(F32), value).astype(BF16), jnp.where(low, value, b.astype(F32)).astype(BF16)

    def into_pair(group, pack):
        def put(n, value):
            cols = tile(n + 3 * group, 128, 128)
            gw[0, :, cols], gw[1, :, cols] = pack(value, gw[0, :, cols], gw[1, :, cols])
        return put

    def cols_of(ref, first=0):
        return lambda n: ref[:, tile(n + first, 128, 128)]

    weight_grad(lambda j: nc[:, j], D, [
        (cols_of(gg), into(lambda n: lax.div(n, 4), lambda n: 12 + lax.rem(n, 4)), 8),
        (cols_of(gu), into(lambda n: lax.div(n, 4), lambda n: 16 + lax.rem(n, 4)), 8),
    ])
    scatter.made(0, 1)

    def put_down(xs, own_half):
        def put(n, value):
            cols = tile(n, 128, 128)
            top, bottom = value[0:256], roll_half(value[256:512])
            a, b = jnp.where(low, top, bottom).astype(BF16), jnp.where(low, bottom, top).astype(BF16)
            if own_half:
                rows = tile(c + 2 * xs, 256, 256)
                gwd[0, rows, cols] = a
                gwd[1, rows, cols] = b
            else:
                gdsend[xs, 0, :, cols] = a
                gdsend[xs, 1, :, cols] = b
        return put

    wait_all(gc_copies)
    gd_copies = []
    for xs in range(2):
        weight_grad(lambda j: hidden[:, pl.ds(pl.multiple_of(j.start + 512 * xs, 128), 128)], 512, [
            (lambda n: ffb[:, tile(n + 3 * (1 - c), 128, 128)], put_down(xs, False), 3),
            (lambda n: ffb[:, tile(n + 3 * c, 128, 128)], put_down(xs, True), 3),
        ])
        gd_copies.append(remote(gdsend.at[xs], gwd.at[:, tile(c + 2 * xs, 256, 256)], 38 + xs, mate))

    small[...] = jnp.zeros_like(small)

    def keep_gain(index, i, gain):
        small[index : index + 1, 0:D] += jnp.where(lax.rem(i, 2) == c, gain, 0.0)

    def keep_sliced(chunk, total):
        for n, value in enumerate(sliced_order(lane_tiles(total))):
            gxb[chunk, 128 * n : 128 * n + 128] = value.astype(BF16)

    def back_heads(weight):
        for t in range(3):
            first, second = tile(3 * c + t, 64, 64), tile(3 * c + t + 6, 64, 64)
            part = None
            for p in range(2):
                rows = jnp.concatenate([weight[p, first], weight[p, second]], axis=0)
                term = dot_t(gxb[:, H * p : H * p + H], rows)
                part = term if part is None else part + term
            gatt[:, 128 * t : 128 * t + 128] = part.astype(BF16)

    def third(i):
        chunk = tile(i, 128, 128)
        upstream = gsend[chunk].astype(F32) + grecv[chunk].astype(F32)
        gv, gain = norm_back(x2[chunk], gains[2:3], upstream)
        total = full[2, chunk].astype(F32) + gv
        gx2[chunk] = total
        keep_sliced(chunk, total)
        keep_gain(2, i, gain)

    repeat(4, third)
    wait_all(gd_copies)
    scatter.made(2, 3)
    back_heads(w_co)
    gmkv = grecv
    copies = []
    for t in range(3):
        attend_back(t, cq, 0, mkv, 0, mkv, 3, p_cross, catt, False, gcq, 3 * c, gmkv, 0, gmkv, 3)
        copies.append(send_head(gcq, t, 14))
        scatter.pump(1 if t else 0)

    mem_copies = pair_partial(lambda k: dot_t(gmkv[:, 0:H], w[0, k, 2 * H : 3 * H]) + dot_t(gmkv[:, H:], w[1, k, 2 * H : 3 * H]), psend.at[1], precv.at[1], 17)

    weight_grad(lambda j: full[1, :, j], D, [
        (cols_of(gmkv), into_pair(2, pack_first), 3), (cols_of(gmkv, 3), into_pair(2, pack_second), 3)])
    scatter.made(4)
    scatter.pump(1)

    wait_all(mix_copies)

    def mixed_block(k, chunk):
        return (x2[chunk] + psend[0, 2 * k + c].astype(F32) + precv[0, k].astype(F32)).astype(BF16)

    msend[0] = mixed_block(1 - x, other)
    mix_out = remote(msend.at[0], mixed.at[x], 19, across)
    mixed[x] = mixed_block(x, own)

    weight_grad(lambda j: cattn[:, j], D, [(cols_of(gxb, 3 * c), into_pair(3, pack_second), 3)])
    wait_all(copies)

    def back_b(n):
        cols = tile(n, 256, 256)
        x2[:, cols] = dot_t(gcq[:, 0:H], w_cq[0, cols]) + dot_t(gcq[:, H:], w_cq[1, cols])

    repeat(3, back_b)

    def second(i):
        chunk = tile(i, 128, 128)
        gv, gain = norm_back(x1[chunk], gains[1:2], x2[chunk])
        total = gx2[chunk] + gv
        gx2[chunk] = total
        keep_sliced(chunk, total)
        keep_gain(1, i, gain)

    repeat(4, second)
    natural_heads(att, attn)
    weight_grad(lambda j: attn[:, j], D, [(cols_of(gxb, 3 * c), into_pair(3, pack_first), 3)])
    scatter.made(5)
    scatter.pump(2)
    back_heads(w_o)
    for t in range(3):
        attend_back(t, qkv, 0, qkv, 3, qkv, 6, p_self, att, True, gg, 0, gg, 3, gu, 0)
        scatter.pump(2)

    for copy in mix_copies:
        copy.wait_send()
    started[:] = [copy for copy in started if not any(copy is done for done in mix_copies)]

    def back_a(k):
        part = dot_t(gg[:, 0:H], w[0, k, 0:H]) + dot_t(gg[:, H : 2 * H], w[1, k, 0:H])
        return part + dot_t(gu[:, 0:H], w[0, k, H : 2 * H])

    ig_copies = pair_partial(back_a, psend.at[0], precv.at[2], 21)

    scatter.pump(1)
    norm(lambda k: full[0, k].astype(F32), 0, na)
    weight_grad(lambda j: na[:, j], D, [
        (cols_of(gg), into_pair(0, pack_first), 3), (cols_of(gg, 3), into_pair(0, pack_second), 3),
        (cols_of(gu), into_pair(1, pack_first), 3)])
    scatter.made(6)
    scatter.pump(1)
    norm(lambda k: x1[k], 1, nb)
    weight_grad(lambda j: nb[:, j], D, [(cols_of(gcq, 3 * c), into_pair(1, pack_second), 3)])
    scatter.made(7)
    scatter.pump(1)

    flipped = (
        lax.broadcasted_iota(jnp.int32, (T, T), 0) + lax.broadcasted_iota(jnp.int32, (T, T), 1) == T - 1
    ).astype(F32)
    by_bucket = (
        jnp.broadcast_to(buckets[...], (128, T)) == lax.broadcasted_iota(jnp.int32, (128, T), 0)
    ).astype(F32)
    high = lax.Precision.HIGHEST
    distances = jnp.dot(dist_grad[...], flipped, precision=high, preferred_element_type=F32)
    per_head = lax.dot_general(
        distances, by_bucket, (((1,), (1,)), ((), ())), precision=high, preferred_element_type=F32)
    for t in range(3):
        for a in range(2):
            here = lax.broadcasted_iota(jnp.int32, (16, 128), 0) == 3 * (2 * a + c) + t
            small[:, D:] += jnp.where(here, per_head[2 * t + a : 2 * t + a + 1], 0.0)

    wait_all(mem_copies)
    msend[1] = (psend[1, 2 * (1 - x) + c].astype(F32) + precv[1, 1 - x].astype(F32)).astype(BF16)
    mem_out = remote(msend.at[1], late.at[0], 20, across)
    memory_grad[x] = psend[1, 2 * x + c].astype(F32) + precv[1, x].astype(F32)

    scatter.pump(2)
    wait_all(ig_copies)

    def first_block(k, chunk):
        upstream = psend[0, 2 * k + c].astype(F32) + precv[2, k].astype(F32)
        gv, gain = norm_back(full[0, chunk].astype(F32), gains[0:1], upstream)
        small[0:1, 0:D] += gain
        return gx2[chunk] + gv

    msend[2] = first_block(1 - x, other).astype(BF16)
    ig_out = remote(msend.at[2], late.at[1], 23, across)
    input_grad[x] = first_block(x, own)

    if inside:
        z, y, _, _ = place()

        def small_send(slot, ref, peer):
            copy = pltpu.make_async_remote_copy(
                src_ref=ref, dst_ref=got.at[slot], send_sem=small_ssem.at[slot], recv_sem=small_rsem.at[slot],
                device_id=peer, device_id_type=MESH)
            copy.start()
            started.append(copy)
            return copy

        held = small
        for slot, peer in enumerate((mate, scatter.x_peer, scatter.y_peer)):
            copy = small_send(slot, held, peer)
            scatter.pump(3)
            copy.wait_recv()
            acc[slot] = held[...] + got[slot]
            held = acc.at[slot]
        last = [small_send(2 + j, held, scatter.z_peers[j - 1]) for j in range(1, 4)]
        scatter.pump(100)
        wait_all(last)
        total[...] = held[...] + got[3] + got[4] + got[5]

    mem_out.wait_recv()
    memory_grad[1 - x] = late[0].astype(F32)
    ig_out.wait_recv()
    input_grad[1 - x] = late[1].astype(F32)
    mix_out.wait_recv()
    for copy in started + weights.sent + scatter.sent:
        copy.wait_send()


def layer(blocks, segments, buckets, pos_bias, packed, inside):
    def bf(*shape):
        return VMEM(shape, BF16)

    def fl(*shape):
        return VMEM(shape, F32)

    blocks_out = [((2, 128, D), BF16), ((2, 128, D), F32), ((2, 128, D), F32)]
    tiny = (16, D + 128)
    if inside:
        outs = blocks_out + [((96, 2560), F32), ((128, H), F32), (tiny, F32)]
    else:
        outs = blocks_out + [(tiny, F32), ((2, D, 2688), BF16), ((2, FH, H), BF16)]
    whole = pl.BlockSpec(memory_space=pltpu.VMEM)
    dma = pltpu.SemaphoreType.DMA
    gather_sems = [dma((len(GATHER), 15)), dma((len(GATHER), 15))] if inside else [dma((2,)), dma((2,))]
    own = [
        fl(*tiny), bf(2, D, 2688), bf(2, FH, H), fl(3, *tiny), fl(6, *tiny),
        bf(2, 4, 96, 2560), bf(2, 4, 128, H), bf(4, 96, 2560), bf(4, 128, H), bf(3, 96, 2560), bf(3, 128, H),
        dma((len(SCATTER), 12)), dma((len(SCATTER), 12)), dma((6,)), dma((6,)),
    ] if inside else []
    return pl.pallas_call(
        functools.partial(layer_kernel, inside),
        out_shape=[jax.ShapeDtypeStruct(s, d) for s, d in outs],
        in_specs=[whole] * 6 + [whole if inside else pl.BlockSpec(memory_space=pl.ANY)] * len(packed),
        out_specs=[whole] * len(outs),
        scratch_shapes=[
            bf(2, D, H), bf(2, D, H), bf(2, D, H), bf(2, 4, 256, H), fl(8, D), fl(8, T), fl(8, T),
            bf(3, T, D), bf(T, D), bf(T, D), bf(T, 3 * H), bf(T, D), bf(T, D), fl(T, D),
            bf(T, H), bf(T, D), bf(T, D), fl(T, D),
            bf(6, T, T), bf(6, 256, 3 * 256), bf(T, FH), bf(T, FH), bf(T, FH), bf(T, D), bf(T, D),
            fl(T, D), bf(T, D),
            bf(T, D), fl(128, T), fl(128, T), bf(128, T), bf(128, T),
            bf(D, T), fl(T, T),
            bf(2, 4, 128, D), bf(3, 2, 128, D), bf(3, 128, D), bf(2, 128, D), bf(2, 2, 256, H),
            pltpu.SemaphoreType.DMA((40,)), pltpu.SemaphoreType.DMA((40,)), *gather_sems, *own,
        ],
        input_output_aliases={},
        compiler_params=pltpu.CompilerParams(
            collective_id=0, has_side_effects=True, vmem_limit_bytes=67043328),
        name="layer",
    )(*blocks, segments, buckets.reshape(1, T), pos_bias, *packed)


PAIRS = ((0, 1), (2, 4), (5, 6), (3, 7))


def pack_pair(a, b, x):
    n = a.shape[0]
    both = jnp.stack([a.reshape(n, 3, 64), b.reshape(n, 3, 64)], axis=2)
    return jnp.where(x == 0, both, both[:, :, ::-1]).reshape(n, H)


def unpack_pair(v, x):
    both = v.reshape(v.shape[0], 3, 2, 64)
    both = jnp.where(x == 0, both, both[:, :, ::-1])
    return both[:, :, 0].reshape(-1, 192), both[:, :, 1].reshape(-1, 192)


def hidden_order(v, half, forward=True):
    n = v.shape[0]
    outer = v.shape[1] // (2 * half)
    v = v.reshape((n, outer, 2, half) if forward else (n, 2, outer, half))
    return v.transpose(0, 2, 1, 3).reshape(n, -1)


def payload(squares, gate, up, down, gains, x):
    half = down.shape[0] // 2
    parts = [pack_pair(squares[a], squares[b], x) for a, b in PAIRS]
    parts += [hidden_order(gate, half), hidden_order(up, half)]
    parts.append(jnp.pad(gains.T, ((0, 0), (0, 125))))
    return jnp.concatenate(parts, axis=1), pack_pair(down[:half], down[half:], x)


def gather_plain(v):
    v = lax.all_gather(v, "rows", axis=0, tiled=True)
    return lax.all_gather(v, "seq", axis=0, axis_index_groups=[[0, 2], [1, 3]])


def finish_kernel(mixed_in, input_in, memory_in, sums, sums_d, small, *outs):
    x = lax.div(lax.axis_index("seq"), 2)
    low = low_lanes()
    mixed, input_grad, memory_grad = outs[:3]
    squares, gate, up, down, gains, bias = outs[3:11], *outs[11:]
    mixed[...] = mixed_in[...]
    input_grad[...] = input_in[...]
    memory_grad[...] = memory_in[...]

    def unpack(value, one, two):
        tiles = [jnp.where(x == 0, v, roll_half(v)) for v in lane_tiles(value)]
        turned = [roll_half(v) for v in tiles]
        one[:, 0:128] = jnp.where(low, tiles[0], turned[1])
        one[:, 128:192] = tiles[2][:, 0:64]
        two[:, 0:128] = jnp.where(low, turned[0], tiles[1])
        two[:, 128:192] = turned[2][:, 0:64]

    for n, (a, b) in enumerate(PAIRS):
        unpack(sums[:, H * n : H * n + H], squares[a], squares[b])
    unpack(sums_d[...], down.at[0:128], down.at[128:256])
    for n, m in enumerate((0, 2, 1, 3)):
        gate[:, 128 * m : 128 * m + 128] = sums[:, 1536 + 128 * n : 1664 + 128 * n]
        up[:, 128 * m : 128 * m + 128] = sums[:, 2048 + 128 * n : 2176 + 128 * n]
    shift = lax.rem(D - 96 * lax.axis_index("rows"), D)
    gains[...] = pltpu.roll(small[0:8, 0:D], shift, 1)[0:3, 0:96]
    bias[...] = small[:, D:].T[0:BUCKETS, 0:HEADS]


def finish(mixed, input_grad, memory_grad, sums, sums_d, small):
    whole = pl.BlockSpec(memory_space=pltpu.VMEM)
    outs = [jax.ShapeDtypeStruct(v.shape, v.dtype) for v in (mixed, input_grad, memory_grad)]
    shapes = [(96, 192)] * 8 + [(96, 512), (96, 512), (256, 192), (3, 96), (BUCKETS, HEADS)]
    outs += [jax.ShapeDtypeStruct(s, F32) for s in shapes]
    return tuple(pl.pallas_call(
        finish_kernel,
        out_shape=outs,
        in_specs=[whole] * 6,
        out_specs=[whole] * len(outs),
        name="finish",
    )(mixed, input_grad, memory_grad, sums, sums_d, small))


def scatter_plain(gw, gwd, small, x):
    gw = gw[:, :, :2560]

    def reduced(v):
        v = lax.psum_scatter(v, "rows", scatter_dimension=1, tiled=True)
        kept = lax.dynamic_index_in_dim(v, x, 0, keepdims=False).astype(F32)
        sent = lax.dynamic_index_in_dim(v, 1 - x, 0, keepdims=False)
        return kept + lax.ppermute(sent, "seq", [(0, 2), (2, 0), (1, 3), (3, 1)]).astype(F32)

    total, down = reduced(gw), reduced(gwd)
    half = down.shape[0]
    squares = [None] * 8
    for k, (a, b) in enumerate(PAIRS):
        squares[a], squares[b] = unpack_pair(total[:, H * k : H * k + H], x)
    gate = hidden_order(total[:, 1536:2048], half, False)
    up = hidden_order(total[:, 2048:], half, False)
    down = jnp.concatenate(unpack_pair(down, x), axis=0)
    return squares, gate, up, down, lax.psum(small, ("rows", "seq"))


def shards(
    layer_input, memory, output_grad, segments, buckets,
    self_query, self_key, self_value, self_output,
    cross_query, cross_key, cross_value, cross_output,
    gate_weight, up_weight, down_weight, norm_gains, position_bias,
):
    x = lax.axis_index("seq") // 2
    squares = (self_query, self_key, self_value, self_output, cross_query, cross_key, cross_value, cross_output)
    inside = lax.axis_size("rows") == 8
    packed = (*squares, gate_weight, up_weight, down_weight, norm_gains)
    if not inside:
        packed = [gather_plain(v) for v in payload(squares, gate_weight, up_weight, down_weight, norm_gains, x)]
    result = layer(
        (layer_input, memory, output_grad), segments, buckets, position_bias, packed, inside)
    if inside:
        return finish(*result)
    mixed, input_grad, memory_grad, small, gw, gwd = result
    squares, gate, up, down, small = scatter_plain(gw, gwd, small, x)
    width = D // lax.axis_size("rows")
    gains = lax.dynamic_slice(small, (0, lax.axis_index("rows") * width), (3, width))
    return (mixed, input_grad, memory_grad, *squares, gate, up, down, gains, small[:HEADS, D : D + BUCKETS].T)


def solution(mesh):
    tokens = P("rows", "seq", None)
    weight = P("rows", "seq")
    return jax.shard_map(
        shards,
        mesh=mesh,
        in_specs=(tokens, tokens, tokens, P("rows", None), P()) + (weight,) * 11 + (P(None, "rows"), P()),
        out_specs=(tokens,) * 3 + (weight,) * 11 + (P(None, "rows"), P()),
        check_vma=False,
    )
```
